512 devices in a mesh: row: 128 (over z, y, core), ex: 4 (over x).
Axes of the slice: x: 4, y: 8, z: 8, core: 2. Of those that a mesh axis runs over, the one named last changes fastest.
Arguments:
- grads: bfloat16 [1, 4, 2048, 2048], P(None, 'ex', 'row'), may hold values from -6 to 6
- right_inv: bfloat16 [2048, 2048], P('row', 'ex'), may hold values from -0.125 to 0.125
- left_inv: bfloat16 [2048, 2048], P(('row', 'ex')), may hold values from -0.125 to 0.125
- row_signs: int32 [1, 4, 2048], replicated, may hold values from 0 to 1
- col_signs: int32 [1, 4, 2048], replicated, may hold values from 0 to 1
- listed: int32 [1, 128, 4, 32], P(None, 'row', 'ex'), may hold values from 0 to 32767, as said below
- owners: int32 [1, 128, 4, 32, 1], P(None, 'row'), may hold values from 0 to 127; in each aligned block of 128 rows (0 to 127, 128 to 255, ..., all dimensions but the last counted through in order) at most 2 rows name the same one
Outputs:
- sketch: float32 [1, 128, 128, 2, 256], P(None, 'row')
The draws below stay inside these ranges and needn't reach their ends.
Inputs may be any that keep to these rules, and one draw needn't show every extreme that they name: `listed`: for each batch b, group g and example x, the 32 entries name distinct blocks in ascending order, all from g * 256 to (g + 1) * 256 - 1. `owners`: within one batch and group, no owner is named by more than 2 of the 128 entries, a bound that some block reaches.
All inputs are finite; a program needn't handle non-finite values.
Results may differ from the reference program's by a relative error of at most 0.0029.
Values may be sent and summed in bfloat16 or wider, within the bound.
No kernel may reach another device: no remote copies, remote signals or barrier semaphores. Data moves between devices by JAX's collectives and lax.ppermute only.
A program may use at most 64 MiB of HBM per device.

```python
import math
import jax
import jax.numpy as jnp
import numpy as np

DM = 2048
BLOCK = 128
NBLK = 16
BATCHES = 1
EXB = 4
GROUPS = 128
BLK_DEV = 256
LIST_DEV = 32
SCAP = 2


def draw_listed(key, part):
    total = BATCHES * GROUPS * EXB
    keys = jax.random.split(jax.random.fold_in(key, 7), total)

    def pick_one(subkey):
        return jnp.sort(jax.random.permutation(subkey, BLK_DEV)[:LIST_DEV])
    chosen = jax.vmap(pick_one)(keys).reshape(BATCHES, GROUPS, EXB, LIST_DEV)
    offsets = (jnp.arange(GROUPS, dtype=jnp.int32) * BLK_DEV)[None, :, None, None]
    return (chosen.astype(jnp.int32) + offsets).astype(jnp.int32)


def with_ends(values, key, smallest, top_value):
    dims = values.shape
    index_at = [jax.random.randint(jax.random.fold_in(key, axis), (), 0, dims[axis]) for axis in range(len(dims))]
    values = values.at[tuple(index_at)].set(smallest)
    longest = dims.index(max(dims))
    index_at[longest] = (index_at[longest] + 1) % dims[longest]
    return values.at[tuple(index_at)].set(top_value)


def block_scale(stream_key, shape, shards, low, largest):
    loudness = 1.0
    for position, parts in shards:
        steps = jax.random.uniform(jax.random.fold_in(jax.random.fold_in(stream_key, 6), position), (parts,), jnp.float32, low / len(shards), largest / len(shards))
        loudness = loudness * jnp.repeat(jnp.exp(steps), shape[position] // parts).reshape((-1,) + (1,) * (len(shape) - 1 - position))
    return loudness


def shared_out(stream_key, own, number, rows, amount, top, most, skew):
    ranking = jax.random.permutation(stream_key, amount)
    crowded, ordinary = portions_of(amount, rows * top, most, skew, True), portions_of(amount, rows * top, most, skew, False)
    places = jnp.arange(amount)

    def named(lengths, turn):
        used = int((lengths > 0).sum())
        fixed = max(1, used // 4)
        passed = fixed + (places - fixed + turn * (used - fixed)) % max(1, amount - fixed)
        return jnp.zeros((amount,), jnp.int32).at[ranking[jnp.where(places < fixed, places, passed)]].set(jnp.asarray(lengths, jnp.int32))

    lengths = jnp.where(number % 4 == 0, named(crowded, number // 4), named(ordinary, number - number // 4 - 1))
    mixed = jax.random.permutation(jax.random.fold_in(own, 3), amount)
    donor, receiver = mixed[0:amount // 2 * 2:2], mixed[1:amount // 2 * 2:2]
    slack = jnp.minimum(lengths[donor] - 1, most - lengths[receiver]) // 2
    slack = jnp.where((donor == ranking[0]) | (receiver == ranking[0]) | (lengths[receiver] == 0), 0, jnp.maximum(slack, 0))
    passed = jax.random.randint(jax.random.fold_in(own, 4), (amount // 2,), 0, 1 << 20) % (slack + 1)
    lengths = lengths.at[donor].add(-passed).at[receiver].add(passed)
    items = jnp.searchsorted(jnp.cumsum(lengths), jnp.arange(rows * top), side="right").astype(jnp.int32)
    listing = items.reshape(top, rows).T
    listing = listing[jax.random.permutation(jax.random.fold_in(own, 1), rows)]
    turn = jax.random.randint(jax.random.fold_in(own, 2), (rows, 1), 0, top)
    return jnp.take_along_axis(listing, (jnp.arange(top)[None, :] + turn) % top, axis=1)


def portions_of(number_of, total, reach, lean, full):
    portions = [(1 << 20) // math.isqrt(grade ** lean) + 1 for grade in range(1, number_of + 1)]
    largest = reach if full else min(reach, max(-(-total // number_of), total * portions[0] // sum(portions)))
    least = 1 if total - largest >= number_of - 1 else 0
    holding, spare = [largest] + [least] * (number_of - 1), total - largest - least * (number_of - 1)
    while spare > 0:
        candidates = [i for i in range(1, number_of) if holding[i] < largest] or [i for i in range(1, number_of) if holding[i] < reach]
        whole, left = sum([portions[i] for i in candidates]), spare
        for i in candidates:
            addition = min(reach - holding[i], max(1, left * portions[i] // whole), spare)
            holding[i] = holding[i] + addition
            spare = spare - addition
    return np.array(holding)


def normal_values(stream_key, dims, spread, most, cuts=(), kind=jnp.bfloat16):
    result = spread * jax.random.normal(stream_key, dims, jnp.float32)
    if cuts:
        result = result * block_scale(stream_key, dims, cuts, -0.22, 0.18)
    return jnp.clip(result, -most, most).astype(kind)


def setup_inputs(seed: int = 0) -> dict:
    seeds = jax.random.split(jax.random.key(seed), 8)
    grads = normal_values(seeds[0], (BATCHES, EXB, DM, DM), 1.0, 6.0, ((1, 4), (2, 128)))
    right_inv = normal_values(seeds[1], (DM, DM), DM ** -0.5, 0.125, ((0, 128), (1, 4)))
    left_inv = normal_values(seeds[2], (DM, DM), DM ** -0.5, 0.125, ((0, 512),))
    row_signs = with_ends(jax.random.randint(seeds[3], (BATCHES, EXB, DM), 0, 2), jax.random.fold_in(seeds[3], 1), 0, 1).astype(jnp.int32)
    col_signs = with_ends(jax.random.randint(seeds[4], (BATCHES, EXB, DM), 0, 2), jax.random.fold_in(seeds[4], 1), 0, 1).astype(jnp.int32)
    listed = draw_listed(jax.random.fold_in(seeds[7], 71), 0)
    owners_keys = jax.random.split(jax.random.fold_in(seeds[6], 1), BATCHES * GROUPS * EXB * LIST_DEV // (EXB * LIST_DEV))
    owners_turns = jax.random.permutation(jax.random.fold_in(seeds[6], 3), BATCHES * GROUPS * EXB * LIST_DEV // (EXB * LIST_DEV))
    owners = jax.vmap(lambda own, number: shared_out(jax.random.fold_in(seeds[6], 2), own, number, EXB * LIST_DEV, GROUPS, 1, SCAP, 2))(owners_keys, owners_turns).reshape((BATCHES, GROUPS, EXB, LIST_DEV, 1))
    return {"grads": grads, "right_inv": right_inv, "left_inv": left_inv, "row_signs": row_signs, "col_signs": col_signs, "listed": listed, "owners": owners}


def reference(grads, right_inv, left_inv, row_signs, col_signs, listed, owners):
    results = []
    for batch_index in range(BATCHES):
        packs = []
        for example in range(EXB):
            projected = jnp.dot(grads[batch_index, example], right_inv, preferred_element_type=jnp.float32).astype(jnp.bfloat16)
            whitened = jnp.dot(left_inv, projected, preferred_element_type=jnp.float32)
            row_flip = (1 - 2 * row_signs[batch_index, example]).astype(jnp.float32)
            col_flip = (1 - 2 * col_signs[batch_index, example]).astype(jnp.float32)
            flipped = whitened * row_flip[:, None] * col_flip[None, :]
            spectrum = jnp.fft.fft(flipped.reshape(-1)) / DM
            blocks = spectrum.reshape(DM, DM).T.reshape(DM * NBLK, BLOCK)
            packs.append(jnp.concatenate([jnp.real(blocks), jnp.imag(blocks)], axis=1))
        packed = jnp.stack(packs)
        chosen = listed[batch_index]
        picked = packed[jnp.arange(EXB)[None, :, None], chosen]
        entries = picked.reshape(GROUPS, EXB * LIST_DEV, 2 * BLOCK)
        owner_ids = owners[batch_index, :, :, :, 0].reshape(GROUPS, EXB * LIST_DEV)
        entry_order = jnp.arange(EXB * LIST_DEV)
        before = entry_order[None, :, None] < entry_order[None, None, :]
        same = owner_ids[:, :, None] == owner_ids[:, None, :]
        slot_index = jnp.sum(same & before, axis=1)
        source = jnp.broadcast_to(jnp.arange(GROUPS)[:, None], owner_ids.shape)
        store = jnp.zeros((GROUPS, GROUPS, SCAP, 2 * BLOCK), jnp.float32)
        store = store.at[owner_ids, source, slot_index].set(entries)
        results.append(store)
    return jnp.stack(results)
```

```python
import math

import jax
import jax.numpy as jnp
import numpy as np
from jax import lax
from jax.experimental import pallas as pl
from jax.experimental.pallas import tpu as pltpu
from jax.sharding import Mesh
from jax.sharding import PartitionSpec as P

DM = 2048
BLOCK = 128
NZ, NY, NC, NE = 8, 8, 2, 4
NYC = NY * NC
ROWS = NZ * NYC
GROUP_ROWS = DM // ROWS
TILE_ROWS = DM // NZ
RADIX = 8
INNER = DM // RADIX
ROOT_HALF = math.sqrt(0.5)

f32 = jnp.float32
bf16 = jnp.bfloat16
ROW_AXES = ("z", "y", "c")


def split_table(table):
    high = table.astype(bf16)
    low = (table - high.astype(np.float64)).astype(bf16)
    return high, low


def dft_angles(rows, cols, length):
    return 2.0 * math.pi * ((np.arange(rows)[:, None] * np.arange(cols)[None, :]) % length) / length


def column_tables():
    angles = dft_angles(INNER, INNER, INNER)
    high, low = split_table(np.concatenate([np.cos(angles), -np.sin(angles)], axis=0))
    angles = dft_angles(INNER, RADIX, DM)
    twiddles = np.concatenate([np.cos(angles), -np.sin(angles)], axis=1).astype(np.float32)
    return high, low, twiddles


def row_tables():
    angles = dft_angles(BLOCK, BLOCK, BLOCK)
    real, imag = np.cos(angles), -np.sin(angles)
    full = np.concatenate(
        [np.concatenate([real, imag], axis=1), np.concatenate([-imag, real], axis=1)], axis=0
    )
    high, low = split_table(full)
    angles = dft_angles(NYC, BLOCK, DM)
    twiddles = np.stack([np.cos(angles), -np.sin(angles)]).astype(np.float32)
    return high, low, twiddles.reshape(2, NYC, 1, BLOCK)


def add(a, b):
    return (a[0] + b[0], a[1] + b[1])


def sub(a, b):
    return (a[0] - b[0], a[1] - b[1])


def mul(a, b):
    return (a[0] * b[0] - a[1] * b[1], a[0] * b[1] + a[1] * b[0])


def minus_i(a):
    return (a[1], -a[0])


def fft4(a, b, c, d):
    even, odd = add(a, c), sub(a, c)
    even2, odd2 = add(b, d), minus_i(sub(b, d))
    return [add(even, even2), add(odd, odd2), sub(even, even2), sub(odd, odd2)]


def fft8(terms):
    even = fft4(terms[0], terms[2], terms[4], terms[6])
    odd = fft4(terms[1], terms[3], terms[5], terms[7])
    one = ((odd[1][0] + odd[1][1]) * ROOT_HALF, (odd[1][1] - odd[1][0]) * ROOT_HALF)
    three = ((odd[3][1] - odd[3][0]) * ROOT_HALF, (odd[3][0] + odd[3][1]) * -ROOT_HALF)
    turned = [odd[0], one, minus_i(odd[2]), three]
    return [add(e, o) for e, o in zip(even, turned)] + [sub(e, o) for e, o in zip(even, turned)]


def fft16(terms):
    inner = [fft4(*[terms[4 * a + b] for a in range(4)]) for b in range(4)]
    out = [None] * 16
    for first in range(4):
        column = []
        for b in range(4):
            turn = -2.0 * math.pi * b * first / 16
            value = inner[b][first]
            if b * first:
                cos, sin = math.cos(turn), math.sin(turn)
                value = (value[0] * cos - value[1] * sin, value[0] * sin + value[1] * cos)
            column.append(value)
        for second, value in enumerate(fft4(*column)):
            out[first + 4 * second] = value
    return out


def dot(a, b):
    return jnp.dot(a, b, preferred_element_type=f32)


def whiten_kernel(gg, rl, lx, row_flip, col_flip, high, low, twiddles, out, white, stage):
    right = rl[:, 0:GROUP_ROWS, :].reshape(DM, BLOCK)
    projected = dot(gg[...].reshape(TILE_ROWS, DM), right) * col_flip[...]
    projected = projected.astype(bf16).reshape(NC, NY, GROUP_ROWS, BLOCK)
    tile = jnp.concatenate([projected[c, y] for y in range(NY) for c in range(NC)], axis=0)
    left = jnp.concatenate([lx[0].reshape(DM, BLOCK), lx[1].reshape(DM, BLOCK)], axis=1)
    white[...] = dot(left, tile) * row_flip[...]
    for p in range(RADIX):
        part = white[pl.ds(p, INNER, stride=RADIX), :]
        part_high = part.astype(bf16)
        part_low = (part - part_high.astype(f32)).astype(bf16)
        stage[p] = dot(high[...], part_high) + dot(low[...], part_high) + dot(high[...], part_low)

    def combine(step, carry):
        rows = pl.ds(pl.multiple_of(step * GROUP_ROWS, GROUP_ROWS), GROUP_ROWS)
        rows_imag = pl.ds(pl.multiple_of(INNER + step * GROUP_ROWS, GROUP_ROWS), GROUP_ROWS)
        factors = twiddles[rows, :]
        terms = [(stage[0, rows, :], stage[0, rows_imag, :])]
        for p in range(1, RADIX):
            factor = (factors[:, p : p + 1], factors[:, RADIX + p : RADIX + p + 1])
            terms.append(mul((stage[p, rows, :], stage[p, rows_imag, :]), factor))
        for k, value in enumerate(fft8(terms)):
            out[NYC * k + step, 0:GROUP_ROWS, :] = value[0].astype(bf16)
            out[NYC * k + step, GROUP_ROWS : 2 * GROUP_ROWS, :] = value[1].astype(bf16)
        return carry

    lax.fori_loop(0, INNER // GROUP_ROWS, combine, 0)


def spectrum_kernel(parts, cross, turns, high, low, chosen, block_of, spread, out, mixed):
    terms = []
    for yc in range(NYC):
        total = parts[yc].astype(f32)
        for z in range(1, NZ):
            total = total + parts[z * NYC + yc].astype(f32)
        terms.append(
            mul((total[0:GROUP_ROWS], total[GROUP_ROWS:]), (cross[0, yc], cross[1, yc]))
        )
    for k, value in enumerate(fft16(terms)):
        value = mul(value, (turns[0, k], turns[1, k]))
        mixed[k, :, 0:BLOCK] = value[0]
        mixed[k, :, BLOCK : 2 * BLOCK] = value[1]
    rows = mixed[...].reshape(NYC * GROUP_ROWS, 2 * BLOCK)
    rows_high = rows.astype(bf16)
    rows_low = (rows - rows_high.astype(f32)).astype(bf16)
    result = dot(rows_high, high[...]) + dot(rows_low, high[...]) + dot(rows_high, low[...])
    picked = dot(chosen[...], result.astype(bf16))
    count = picked.shape[0] // NYC
    lane_block = lax.broadcasted_iota(jnp.int32, (NYC * count, BLOCK), 1) // (BLOCK // NYC)
    keep = lane_block == block_of[...]
    sides = []
    for side in range(2):
        own = jnp.where(keep, picked[:, side * BLOCK : (side + 1) * BLOCK], 0.0).astype(bf16)
        own = own.reshape(NYC, count, BLOCK)
        wide = jnp.concatenate([own[k] for k in range(NYC)], axis=1)
        sides.append(dot(wide, spread[...]))
    out[...] = jnp.concatenate(sides, axis=1).astype(bf16)


def shards(grads, right_inv, left_inv, row_signs, col_signs, listed, owners):
    z_id, y_id, c_id, e_id = (lax.axis_index(name) for name in ("z", "y", "c", "e"))
    yc_id = y_id * NC + c_id
    row_id = z_id * NYC + yc_id
    list_len = listed.shape[3]
    capacity = 2

    right_pieces = right_inv.reshape(GROUP_ROWS, NE, BLOCK).transpose(1, 0, 2)
    left_pieces = left_inv.reshape(NE, NYC, BLOCK).transpose(1, 0, 2)
    shared = jnp.concatenate(
        [right_pieces.reshape(NE * GROUP_ROWS, BLOCK), left_pieces.reshape(NYC * NE, BLOCK)], axis=0
    )
    shared = jnp.broadcast_to(shared[None], (NE,) + shared.shape)
    shared = lax.all_to_all(shared, "e", 0, 0, tiled=True)
    right_all = shared[:, : NE * GROUP_ROWS].reshape(NYC, GROUP_ROWS, BLOCK)
    left_all = shared[:, NE * GROUP_ROWS :].reshape(NE, NYC, NE, BLOCK).transpose(1, 0, 2, 3)
    left_all = left_all.reshape(NZ, 1, NC, GROUP_ROWS, BLOCK)
    right_all = right_all.reshape(1, NY, NC, GROUP_ROWS, BLOCK)
    whole = (NZ, NY, NC, GROUP_ROWS, BLOCK)
    factors = jnp.concatenate(
        [jnp.broadcast_to(right_all, whole), jnp.broadcast_to(left_all, whole)], axis=3
    ).reshape(ROWS, 2 * GROUP_ROWS, BLOCK)
    factors = lax.all_to_all(factors, ROW_AXES, 0, 0, tiled=True)

    rows = jnp.broadcast_to(grads.reshape(1, GROUP_ROWS, DM), (NY, GROUP_ROWS, DM))
    rows = lax.all_to_all(rows, "y", 0, 0, tiled=True)
    rows = lax.all_to_all(
        jnp.broadcast_to(rows[None], (NC,) + rows.shape), "c", 0, 0, tiled=True
    )
    left_half = factors[:, GROUP_ROWS:]
    left_cols = lax.all_to_all(
        jnp.broadcast_to(left_half[None], (NC,) + left_half.shape), "c", 0, 0, tiled=True
    )

    row_bits = lax.dynamic_index_in_dim(row_signs[0], e_id, 0, keepdims=False)
    col_bits = lax.dynamic_slice(col_signs[0], (e_id, yc_id * BLOCK), (1, BLOCK))
    row_flip = (1 - 2 * row_bits).astype(f32)[:, None]
    col_flip = (1 - 2 * col_bits).astype(f32)
    high, low, twiddles = column_tables()
    partial_cols = pl.pallas_call(
        whiten_kernel,
        out_shape=jax.ShapeDtypeStruct((ROWS, 2 * GROUP_ROWS, BLOCK), bf16),
        scratch_shapes=[
            pltpu.VMEM((DM, BLOCK), f32),
            pltpu.VMEM((RADIX, 2 * INNER, BLOCK), f32),
        ],
        name="whiten",
    )(rows, factors, left_cols, row_flip, col_flip, high, low, twiddles)
    partial_rows = lax.all_to_all(partial_cols, ROW_AXES, 0, 0, tiled=True)

    spectrum_rows = row_id * GROUP_ROWS + jnp.arange(GROUP_ROWS, dtype=jnp.int32)
    columns = jnp.arange(DM, dtype=jnp.int32).reshape(NYC, 1, BLOCK)
    phase = spectrum_rows[None, :, None] * columns
    angle = phase.astype(f32) * (2.0 * math.pi / (DM * DM))
    cross = jnp.stack([jnp.cos(angle), -jnp.sin(angle)]) * (1.0 / DM)
    local_ids = listed[0, 0, 0] - row_id * (GROUP_ROWS * NYC)
    lane_row = jnp.arange(NYC * GROUP_ROWS, dtype=jnp.int32)
    chosen = (
        (lane_row // GROUP_ROWS)[None, None, :] == jnp.arange(NYC, dtype=jnp.int32)[:, None, None]
    ) & ((lane_row % GROUP_ROWS)[None, None, :] == (local_ids // NYC)[None, :, None])
    chosen = chosen.reshape(NYC * list_len, NYC * GROUP_ROWS).astype(bf16)
    block_of = jnp.tile(local_ids % NYC, NYC)[:, None]
    source = jnp.arange(NYC * BLOCK, dtype=jnp.int32)
    target = NYC * (source % (BLOCK // NYC)) + source // BLOCK
    spread = (target[:, None] == jnp.arange(BLOCK, dtype=jnp.int32)[None, :]).astype(bf16)
    row_high, row_low, turns = row_tables()
    picked = pl.pallas_call(
        spectrum_kernel,
        out_shape=jax.ShapeDtypeStruct((list_len, 2 * BLOCK), bf16),
        scratch_shapes=[pltpu.VMEM((NYC, GROUP_ROWS, 2 * BLOCK), f32)],
        name="spectrum",
    )(partial_rows, cross, turns, row_high, row_low, chosen, block_of, spread)

    entries = lax.all_to_all(
        jnp.broadcast_to(picked[None], (NE,) + picked.shape), "e", 0, 0, tiled=True
    ).reshape(NE * list_len, 2 * BLOCK)
    owner_ids = owners[0, 0, :, :, 0].reshape(-1)
    order = jnp.arange(NE * list_len, dtype=jnp.int32)
    same = (owner_ids[:, None] == owner_ids[None, :]) & (order[:, None] < order[None, :])
    position = owner_ids * capacity + jnp.sum(same.astype(jnp.int32), axis=0)
    place = jnp.arange(ROWS * capacity, dtype=jnp.int32)[:, None] == position[None, :]
    outgoing = dot(place.astype(bf16), entries).astype(bf16)
    outgoing = outgoing.reshape(ROWS, capacity, 2 * BLOCK)
    arrived = lax.all_to_all(outgoing, ROW_AXES, 0, 0, tiled=True)
    return arrived.astype(f32)[None, None]


def solution(mesh):
    split = Mesh(mesh.devices.reshape(NZ, NY, NC, NE), ("z", "y", "c", "e"))
    in_specs = (
        P(None, "e", ROW_AXES, None),
        P(ROW_AXES, "e"),
        P(ROW_AXES + ("e",), None),
        P(),
        P(),
        P(None, ROW_AXES, "e", None),
        P(None, ROW_AXES, None, None, None),
    )
    out_specs = P(None, ROW_AXES, None, None, None)
    return jax.shard_map(shards, mesh=split, in_specs=in_specs, out_specs=out_specs, check_vma=False)
```

```python
import math

import jax
import jax.numpy as jnp
import numpy as np
from jax import lax
from jax.experimental import pallas as pl
from jax.experimental.pallas import tpu as pltpu
from jax.sharding import Mesh
from jax.sharding import PartitionSpec as P

DM = 2048
BLOCK = 128
NZ, NY, NC, NE = 8, 8, 2, 4
NYC = NY * NC
ROWS = NZ * NYC
GROUP_ROWS = DM // ROWS
TILE_ROWS = DM // NZ
RADIX = 8
INNER = DM // RADIX
ROOT_HALF = math.sqrt(0.5)

f32 = jnp.float32
bf16 = jnp.bfloat16
ROW_AXES = ("z", "y", "c")
IN_VMEM = pl.BlockSpec(memory_space=pltpu.VMEM)
IN_SMEM = pl.BlockSpec(memory_space=pltpu.SMEM)


def split_table(table):
    high = table.astype(bf16)
    low = (table - high.astype(np.float64)).astype(bf16)
    return high, low


def dft_angles(rows, cols, length):
    return 2.0 * math.pi * ((np.arange(rows)[:, None] * np.arange(cols)[None, :]) % length) / length


def column_tables():
    angles = dft_angles(INNER, INNER, INNER)
    high, low = split_table(np.concatenate([np.cos(angles), -np.sin(angles)], axis=0))
    angles = dft_angles(INNER, RADIX, DM)
    twiddles = np.concatenate([np.cos(angles), -np.sin(angles)], axis=1).astype(np.float32)
    return high, low, twiddles


def row_tables():
    angles = dft_angles(BLOCK, BLOCK, BLOCK)
    real, imag = np.cos(angles), -np.sin(angles)
    full = np.concatenate(
        [np.concatenate([real, imag], axis=1), np.concatenate([-imag, real], axis=1)], axis=0
    )
    high, low = split_table(full)
    angles = dft_angles(NYC, BLOCK, DM)
    twiddles = np.stack([np.cos(angles), -np.sin(angles)]).astype(np.float32)
    return high, low, twiddles.reshape(2, NYC, 1, BLOCK)


def add(a, b):
    return (a[0] + b[0], a[1] + b[1])


def sub(a, b):
    return (a[0] - b[0], a[1] - b[1])


def mul(a, b):
    return (a[0] * b[0] - a[1] * b[1], a[0] * b[1] + a[1] * b[0])


def minus_i(a):
    return (a[1], -a[0])


def fft4(a, b, c, d):
    even, odd = add(a, c), sub(a, c)
    even2, odd2 = add(b, d), minus_i(sub(b, d))
    return [add(even, even2), add(odd, odd2), sub(even, even2), sub(odd, odd2)]


def fft8(terms):
    even = fft4(terms[0], terms[2], terms[4], terms[6])
    odd = fft4(terms[1], terms[3], terms[5], terms[7])
    one = ((odd[1][0] + odd[1][1]) * ROOT_HALF, (odd[1][1] - odd[1][0]) * ROOT_HALF)
    three = ((odd[3][1] - odd[3][0]) * ROOT_HALF, (odd[3][0] + odd[3][1]) * -ROOT_HALF)
    turned = [odd[0], one, minus_i(odd[2]), three]
    return [add(e, o) for e, o in zip(even, turned)] + [sub(e, o) for e, o in zip(even, turned)]


def fft16(terms):
    inner = [fft4(*[terms[4 * a + b] for a in range(4)]) for b in range(4)]
    out = [None] * 16
    for first in range(4):
        column = []
        for b in range(4):
            turn = -2.0 * math.pi * b * first / 16
            value = inner[b][first]
            if b * first:
                cos, sin = math.cos(turn), math.sin(turn)
                value = (value[0] * cos - value[1] * sin, value[0] * sin + value[1] * cos)
            column.append(value)
        for second, value in enumerate(fft4(*column)):
            out[first + 4 * second] = value
    return out


def dot(a, b):
    return jnp.dot(a, b, preferred_element_type=f32)


def project_kernel(place, own, other, rl, col_flip, out):
    right = rl[:, 0:GROUP_ROWS, :].reshape(DM, BLOCK)
    for side, rows in enumerate((own, other)):
        part = dot(rows[...].reshape(TILE_ROWS // NC, DM), right) * col_flip[...]
        part = part.astype(bf16).reshape(NY, GROUP_ROWS, BLOCK)
        for j in range(NY):
            start = pl.multiple_of(place[NY * side + j], GROUP_ROWS)
            out[pl.ds(start, GROUP_ROWS), :] = part[j]


def whiten_kernel(place, tile, rl, lx, row_flip, high, low, twiddles, out, white, stage):
    left = jnp.concatenate(
        [rl[:, GROUP_ROWS:, :].reshape(DM, BLOCK), lx[...].reshape(DM, BLOCK)], axis=1
    )
    half = TILE_ROWS // NC
    halves = [tile[pl.ds(pl.multiple_of(place[k], half), half), :] for k in range(NC)]
    white[...] = dot(left, jnp.concatenate(halves, axis=0)) * row_flip[...]
    for p in range(RADIX):
        part = white[pl.ds(p, INNER, stride=RADIX), :]
        part_high = part.astype(bf16)
        part_low = (part - part_high.astype(f32)).astype(bf16)
        stage[p] = dot(high[...], part_high) + dot(low[...], part_high) + dot(high[...], part_low)

    def combine(step, carry):
        rows = pl.ds(pl.multiple_of(step * GROUP_ROWS, GROUP_ROWS), GROUP_ROWS)
        rows_imag = pl.ds(pl.multiple_of(INNER + step * GROUP_ROWS, GROUP_ROWS), GROUP_ROWS)
        factors = twiddles[rows, :]
        terms = [(stage[0, rows, :], stage[0, rows_imag, :])]
        for p in range(1, RADIX):
            factor = (factors[:, p : p + 1], factors[:, RADIX + p : RADIX + p + 1])
            terms.append(mul((stage[p, rows, :], stage[p, rows_imag, :]), factor))
        for k, value in enumerate(fft8(terms)):
            out[NYC * k + step, 0:GROUP_ROWS, :] = value[0].astype(bf16)
            out[NYC * k + step, GROUP_ROWS : 2 * GROUP_ROWS, :] = value[1].astype(bf16)
        return carry

    lax.fori_loop(0, INNER // GROUP_ROWS, combine, 0)


def spectrum_kernel(parts, cross, turns, high, low, chosen, block_of, spread, out, mixed):
    terms = []
    for yc in range(NYC):
        total = parts[yc].astype(f32)
        for z in range(1, NZ):
            total = total + parts[z * NYC + yc].astype(f32)
        terms.append(
            mul((total[0:GROUP_ROWS], total[GROUP_ROWS:]), (cross[0, yc], cross[1, yc]))
        )
    for k, value in enumerate(fft16(terms)):
        value = mul(value, (turns[0, k], turns[1, k]))
        mixed[k, :, 0:BLOCK] = value[0]
        mixed[k, :, BLOCK : 2 * BLOCK] = value[1]
    rows = mixed[...].reshape(NYC * GROUP_ROWS, 2 * BLOCK)
    rows_high = rows.astype(bf16)
    rows_low = (rows - rows_high.astype(f32)).astype(bf16)
    result = dot(rows_high, high[...]) + dot(rows_low, high[...]) + dot(rows_high, low[...])
    picked = dot(chosen[...], result.astype(bf16))
    count = picked.shape[0] // NYC
    lane_block = lax.broadcasted_iota(jnp.int32, (NYC * count, BLOCK), 1) // (BLOCK // NYC)
    keep = lane_block == block_of[...]
    sides = []
    for side in range(2):
        own = jnp.where(keep, picked[:, side * BLOCK : (side + 1) * BLOCK], 0.0).astype(bf16)
        own = own.reshape(NYC, count, BLOCK)
        wide = jnp.concatenate([own[k] for k in range(NYC)], axis=1)
        sides.append(dot(wide, spread[...]))
    out[...] = jnp.concatenate(sides, axis=1).astype(bf16)


def shards(grads, right_inv, left_inv, row_signs, col_signs, listed, owners):
    z_id, y_id, c_id, e_id = (lax.axis_index(name) for name in ("z", "y", "c", "e"))
    yc_id = y_id * NC + c_id
    row_id = z_id * NYC + yc_id
    list_len = listed.shape[3]
    capacity = 2

    right_pieces = right_inv.reshape(GROUP_ROWS, NE, BLOCK).transpose(1, 0, 2)
    left_pieces = left_inv.reshape(NE, NYC, BLOCK).transpose(1, 0, 2)
    shared = jnp.concatenate(
        [right_pieces.reshape(NE * GROUP_ROWS, BLOCK), left_pieces.reshape(NYC * NE, BLOCK)], axis=0
    )
    shared = jnp.broadcast_to(shared[None], (NE,) + shared.shape)
    shared = lax.all_to_all(shared, "e", 0, 0, tiled=True)
    right_all = shared[:, : NE * GROUP_ROWS].reshape(NYC, GROUP_ROWS, BLOCK)
    left_all = shared[:, NE * GROUP_ROWS :].reshape(NE, NYC, NE, BLOCK).transpose(1, 0, 2, 3)
    left_all = left_all.reshape(NZ, 1, NC, GROUP_ROWS, BLOCK)
    right_all = right_all.reshape(1, NY, NC, GROUP_ROWS, BLOCK)
    whole = (NZ, NY, NC, GROUP_ROWS, BLOCK)
    factors = jnp.concatenate(
        [jnp.broadcast_to(right_all, whole), jnp.broadcast_to(left_all, whole)], axis=3
    ).reshape(ROWS, 2 * GROUP_ROWS, BLOCK)
    factors = lax.all_to_all(factors, ROW_AXES, 0, 0, tiled=True)

    mine = grads.reshape(GROUP_ROWS, DM)
    up, down = [mine], [mine]
    for _ in range(NY // 2):
        up.append(lax.ppermute(up[-1], "y", [(i, (i + 1) % NY) for i in range(NY)]))
    for _ in range(NY // 2 - 1):
        down.append(lax.ppermute(down[-1], "y", [((i + 1) % NY, i) for i in range(NY)]))
    rows_own = jnp.stack(up + down[1:])
    swap = [(0, 1), (1, 0)]
    rows_other = lax.ppermute(rows_own, "c", swap)
    left_other = lax.ppermute(factors[:, GROUP_ROWS:], "c", swap)
    shift = jnp.array([0, -1, -2, -3, -4, 1, 2, 3], jnp.int32)
    from_y = (y_id + shift) % NY
    row_place = jnp.concatenate(
        [GROUP_ROWS * (NC * from_y + c_id), GROUP_ROWS * (NC * from_y + 1 - c_id)]
    )
    half_place = (TILE_ROWS // NC) * jnp.stack([c_id, 1 - c_id])

    row_bits = lax.dynamic_index_in_dim(row_signs[0], e_id, 0, keepdims=False)
    col_bits = lax.dynamic_slice(col_signs[0], (e_id, yc_id * BLOCK), (1, BLOCK))
    row_flip = (1 - 2 * row_bits).astype(f32)[:, None]
    col_flip = (1 - 2 * col_bits).astype(f32)
    high, low, twiddles = column_tables()
    tile = pl.pallas_call(
        project_kernel,
        out_shape=jax.ShapeDtypeStruct((TILE_ROWS, BLOCK), bf16),
        in_specs=[IN_SMEM] + [IN_VMEM] * 4,
        out_specs=IN_VMEM,
        name="project",
    )(row_place, rows_own, rows_other, factors, col_flip)
    partial_cols = pl.pallas_call(
        whiten_kernel,
        out_shape=jax.ShapeDtypeStruct((ROWS, 2 * GROUP_ROWS, BLOCK), bf16),
        in_specs=[IN_SMEM] + [IN_VMEM] * 7,
        out_specs=IN_VMEM,
        scratch_shapes=[
            pltpu.VMEM((DM, BLOCK), f32),
            pltpu.VMEM((RADIX, 2 * INNER, BLOCK), f32),
        ],
        name="whiten",
    )(half_place, tile, factors, left_other, row_flip, high, low, twiddles)
    partial_rows = lax.all_to_all(partial_cols, ROW_AXES, 0, 0, tiled=True)

    spectrum_rows = row_id * GROUP_ROWS + jnp.arange(GROUP_ROWS, dtype=jnp.int32)
    columns = jnp.arange(DM, dtype=jnp.int32).reshape(NYC, 1, BLOCK)
    phase = spectrum_rows[None, :, None] * columns
    angle = phase.astype(f32) * (2.0 * math.pi / (DM * DM))
    cross = jnp.stack([jnp.cos(angle), -jnp.sin(angle)]) * (1.0 / DM)
    local_ids = listed[0, 0, 0] - row_id * (GROUP_ROWS * NYC)
    lane_row = jnp.arange(NYC * GROUP_ROWS, dtype=jnp.int32)
    chosen = (
        (lane_row // GROUP_ROWS)[None, None, :] == jnp.arange(NYC, dtype=jnp.int32)[:, None, None]
    ) & ((lane_row % GROUP_ROWS)[None, None, :] == (local_ids // NYC)[None, :, None])
    chosen = chosen.reshape(NYC * list_len, NYC * GROUP_ROWS).astype(bf16)
    block_of = jnp.tile(local_ids % NYC, NYC)[:, None]
    source = jnp.arange(NYC * BLOCK, dtype=jnp.int32)
    target = NYC * (source % (BLOCK // NYC)) + source // BLOCK
    spread = (target[:, None] == jnp.arange(BLOCK, dtype=jnp.int32)[None, :]).astype(bf16)
    row_high, row_low, turns = row_tables()
    picked = pl.pallas_call(
        spectrum_kernel,
        out_shape=jax.ShapeDtypeStruct((list_len, 2 * BLOCK), bf16),
        in_specs=[IN_VMEM] * 8,
        out_specs=IN_VMEM,
        scratch_shapes=[pltpu.VMEM((NYC, GROUP_ROWS, 2 * BLOCK), f32)],
        name="spectrum",
    )(partial_rows, cross, turns, row_high, row_low, chosen, block_of, spread)

    entries = lax.all_to_all(
        jnp.broadcast_to(picked[None], (NE,) + picked.shape), "e", 0, 0, tiled=True
    ).reshape(NE * list_len, 2 * BLOCK)
    owner_ids = owners[0, 0, :, :, 0].reshape(-1)
    order = jnp.arange(NE * list_len, dtype=jnp.int32)
    same = (owner_ids[:, None] == owner_ids[None, :]) & (order[:, None] < order[None, :])
    position = owner_ids * capacity + jnp.sum(same.astype(jnp.int32), axis=0)
    place = jnp.arange(ROWS * capacity, dtype=jnp.int32)[:, None] == position[None, :]
    outgoing = dot(place.astype(bf16), entries).astype(bf16)
    outgoing = outgoing.reshape(ROWS, capacity, 2 * BLOCK)
    arrived = lax.all_to_all(outgoing, ROW_AXES, 0, 0, tiled=True)
    return arrived.astype(f32)[None, None]


def solution(mesh):
    split = Mesh(mesh.devices.reshape(NZ, NY, NC, NE), ("z", "y", "c", "e"))
    in_specs = (
        P(None, "e", ROW_AXES, None),
        P(ROW_AXES, "e"),
        P(ROW_AXES + ("e",), None),
        P(),
        P(),
        P(None, ROW_AXES, "e", None),
        P(None, ROW_AXES, None, None, None),
    )
    out_specs = P(None, ROW_AXES, None, None, None)
    return jax.shard_map(shards, mesh=split, in_specs=in_specs, out_specs=out_specs, check_vma=False)
```

```python
import math

import jax
import jax.numpy as jnp
import numpy as np
from jax import lax
from jax.experimental import pallas as pl
from jax.experimental.pallas import tpu as pltpu
from jax.sharding import Mesh
from jax.sharding import PartitionSpec as P

DM = 2048
BLOCK = 128
NZ, NY, NC, NE = 8, 8, 2, 4
NYC = NY * NC
ROWS = NZ * NYC
GROUP_ROWS = DM // ROWS
TILE_ROWS = DM // NZ
RADIX = 8
INNER = DM // RADIX
ROOT_HALF = math.sqrt(0.5)

f32 = jnp.float32
bf16 = jnp.bfloat16
ROW_AXES = ("z", "y", "c")
IN_VMEM = pl.BlockSpec(memory_space=pltpu.VMEM)
IN_SMEM = pl.BlockSpec(memory_space=pltpu.SMEM)


def split_table(table):
    high = table.astype(bf16)
    low = (table - high.astype(np.float64)).astype(bf16)
    return high, low


def dft_angles(rows, cols, length):
    return 2.0 * math.pi * ((np.arange(rows)[:, None] * np.arange(cols)[None, :]) % length) / length


def column_tables():
    angles = dft_angles(INNER, INNER, INNER)
    high, low = split_table(np.concatenate([np.cos(angles), -np.sin(angles)], axis=0))
    angles = dft_angles(INNER, RADIX, DM)
    twiddles = np.concatenate([np.cos(angles), -np.sin(angles)], axis=1).astype(np.float32)
    return high, low, twiddles


def row_tables():
    angles = dft_angles(BLOCK, BLOCK, BLOCK)
    real, imag = np.cos(angles), -np.sin(angles)
    full = np.concatenate(
        [np.concatenate([real, imag], axis=1), np.concatenate([-imag, real], axis=1)], axis=0
    )
    high, low = split_table(full)
    angles = dft_angles(NYC, BLOCK, DM)
    twiddles = np.stack([np.cos(angles), -np.sin(angles)]).astype(np.float32)
    return high, low, twiddles.reshape(2, NYC, 1, BLOCK)


def add(a, b):
    return (a[0] + b[0], a[1] + b[1])


def sub(a, b):
    return (a[0] - b[0], a[1] - b[1])


def mul(a, b):
    return (a[0] * b[0] - a[1] * b[1], a[0] * b[1] + a[1] * b[0])


def minus_i(a):
    return (a[1], -a[0])


def fft4(a, b, c, d):
    even, odd = add(a, c), sub(a, c)
    even2, odd2 = add(b, d), minus_i(sub(b, d))
    return [add(even, even2), add(odd, odd2), sub(even, even2), sub(odd, odd2)]


def fft8(terms):
    even = fft4(terms[0], terms[2], terms[4], terms[6])
    odd = fft4(terms[1], terms[3], terms[5], terms[7])
    one = ((odd[1][0] + odd[1][1]) * ROOT_HALF, (odd[1][1] - odd[1][0]) * ROOT_HALF)
    three = ((odd[3][1] - odd[3][0]) * ROOT_HALF, (odd[3][0] + odd[3][1]) * -ROOT_HALF)
    turned = [odd[0], one, minus_i(odd[2]), three]
    return [add(e, o) for e, o in zip(even, turned)] + [sub(e, o) for e, o in zip(even, turned)]


def fft16(terms):
    inner = [fft4(*[terms[4 * a + b] for a in range(4)]) for b in range(4)]
    out = [None] * 16
    for first in range(4):
        column = []
        for b in range(4):
            turn = -2.0 * math.pi * b * first / 16
            value = inner[b][first]
            if b * first:
                cos, sin = math.cos(turn), math.sin(turn)
                value = (value[0] * cos - value[1] * sin, value[0] * sin + value[1] * cos)
            column.append(value)
        for second, value in enumerate(fft4(*column)):
            out[first + 4 * second] = value
    return out


def dot(a, b):
    return jnp.dot(a, b, preferred_element_type=f32)


def arrange_kernel(pieces, right, left):
    quarter = GROUP_ROWS // NE
    first = lax.broadcasted_iota(jnp.int32, (ROWS, 2 * quarter, BLOCK), 1) < quarter
    rights, lefts = [], []
    for e in range(0, NE, 2):
        even, odd = pieces[e].astype(f32), pieces[e + 1].astype(f32)
        rights.append(jnp.where(first, even, pltpu.roll(odd, quarter, axis=1)))
        lefts.append(jnp.where(first, pltpu.roll(even, quarter, axis=1), odd))
    right[...] = jnp.concatenate(rights, axis=1).astype(bf16)
    left[...] = jnp.concatenate(lefts, axis=1).astype(bf16)


def project_kernel(place, own, other, right, col_flip, out):
    factor = right[...].reshape(DM, BLOCK)
    for side, rows in enumerate((own, other)):
        part = dot(rows[...].reshape(TILE_ROWS // NC, DM), factor) * col_flip[...]
        part = part.astype(bf16).reshape(NY, GROUP_ROWS, BLOCK)
        for y in range(NY):
            start = pl.multiple_of(place[side] + NC * GROUP_ROWS * y, GROUP_ROWS)
            out[pl.ds(start, GROUP_ROWS), :] = part[y]


def whiten_kernel(place, tile, own, other, row_flip, high, low, twiddles, out, white, stage):
    left = jnp.concatenate([own[...].reshape(DM, BLOCK), other[...].reshape(DM, BLOCK)], axis=1)
    half = TILE_ROWS // NC
    halves = [tile[pl.ds(pl.multiple_of(place[k], half), half), :] for k in range(NC)]
    white[...] = dot(left, jnp.concatenate(halves, axis=0)) * row_flip[...]
    for p in range(RADIX):
        part = white[pl.ds(p, INNER, stride=RADIX), :]
        part_high = part.astype(bf16)
        part_low = (part - part_high.astype(f32)).astype(bf16)
        stage[p] = dot(high[...], part_high) + dot(low[...], part_high) + dot(high[...], part_low)

    def combine(step, carry):
        rows = pl.ds(pl.multiple_of(step * GROUP_ROWS, GROUP_ROWS), GROUP_ROWS)
        rows_imag = pl.ds(pl.multiple_of(INNER + step * GROUP_ROWS, GROUP_ROWS), GROUP_ROWS)
        factors = twiddles[rows, :]
        terms = [(stage[0, rows, :], stage[0, rows_imag, :])]
        for p in range(1, RADIX):
            factor = (factors[:, p : p + 1], factors[:, RADIX + p : RADIX + p + 1])
            terms.append(mul((stage[p, rows, :], stage[p, rows_imag, :]), factor))
        for k, value in enumerate(fft8(terms)):
            out[NYC * k + step, 0:GROUP_ROWS, :] = value[0].astype(bf16)
            out[NYC * k + step, GROUP_ROWS : 2 * GROUP_ROWS, :] = value[1].astype(bf16)
        return carry

    lax.fori_loop(0, INNER // GROUP_ROWS, combine, 0)


def spectrum_kernel(parts, cross, turns, high, low, chosen, block_of, spread, out, mixed):
    terms = []
    for yc in range(NYC):
        total = parts[yc].astype(f32)
        for z in range(1, NZ):
            total = total + parts[z * NYC + yc].astype(f32)
        terms.append(
            mul((total[0:GROUP_ROWS], total[GROUP_ROWS:]), (cross[0, yc], cross[1, yc]))
        )
    for k, value in enumerate(fft16(terms)):
        value = mul(value, (turns[0, k], turns[1, k]))
        mixed[k, :, 0:BLOCK] = value[0]
        mixed[k, :, BLOCK : 2 * BLOCK] = value[1]
    rows = mixed[...].reshape(NYC * GROUP_ROWS, 2 * BLOCK)
    rows_high = rows.astype(bf16)
    rows_low = (rows - rows_high.astype(f32)).astype(bf16)
    result = dot(rows_high, high[...]) + dot(rows_low, high[...]) + dot(rows_high, low[...])
    picked = dot(chosen[...], result.astype(bf16))
    count = picked.shape[0] // NYC
    lane_block = lax.broadcasted_iota(jnp.int32, (NYC * count, BLOCK), 1) // (BLOCK // NYC)
    keep = lane_block == block_of[...]
    sides = []
    for side in range(2):
        own = jnp.where(keep, picked[:, side * BLOCK : (side + 1) * BLOCK], 0.0).astype(bf16)
        own = own.reshape(NYC, count, BLOCK)
        wide = jnp.concatenate([own[k] for k in range(NYC)], axis=1)
        sides.append(dot(wide, spread[...]))
    out[...] = jnp.concatenate(sides, axis=1).astype(bf16)


def near(array):
    return pltpu.with_memory_space_constraint(array, pltpu.VMEM)


def shards(grads, right_inv, left_inv, row_signs, col_signs, listed, owners):
    z_id, y_id, c_id, e_id = (lax.axis_index(name) for name in ("z", "y", "c", "e"))
    yc_id = y_id * NC + c_id
    row_id = z_id * NYC + yc_id
    list_len = listed.shape[3]
    capacity = 2

    quarter = GROUP_ROWS // NE
    right_rows = right_inv.reshape(NE, quarter, NE, BLOCK).transpose(0, 2, 1, 3)
    right_rows = lax.all_to_all(right_rows, "e", 0, 0, tiled=True)
    right_rows = right_rows.reshape(1, NY, NC, quarter, BLOCK)
    left_rows = left_inv.reshape(quarter, NYC, BLOCK).transpose(1, 0, 2)
    left_rows = left_rows.reshape(NZ, 1, NC, quarter, BLOCK)
    whole = (NZ, NY, NC, quarter, BLOCK)
    pieces = jnp.concatenate(
        [jnp.broadcast_to(right_rows, whole), jnp.broadcast_to(left_rows, whole)], axis=3
    ).reshape(ROWS, 2 * quarter, BLOCK)
    pieces = lax.all_to_all(pieces, ROW_AXES, 0, 0, tiled=True)
    pieces = lax.all_to_all(jnp.broadcast_to(pieces[None], (NE,) + pieces.shape), "e", 0, 0, tiled=True)

    rows_own = jnp.broadcast_to(grads.reshape(1, GROUP_ROWS, DM), (NY, GROUP_ROWS, DM))
    rows_own = lax.all_to_all(rows_own, "y", 0, 0, tiled=True)
    swap = [(0, 1), (1, 0)]
    rows_other = lax.ppermute(rows_own, "c", swap)
    factor_shape = pltpu.VMEM((ROWS, GROUP_ROWS, BLOCK), bf16)
    right_cols, left_own = pl.pallas_call(
        arrange_kernel,
        out_shape=(factor_shape, factor_shape),
        in_specs=[IN_VMEM],
        out_specs=(IN_VMEM, IN_VMEM),
        name="arrange",
    )(near(pieces))
    left_other = lax.ppermute(left_own, "c", swap)
    sides = jnp.stack([c_id, 1 - c_id])

    row_bits = lax.dynamic_index_in_dim(row_signs[0], e_id, 0, keepdims=False)
    col_bits = lax.dynamic_slice(col_signs[0], (e_id, yc_id * BLOCK), (1, BLOCK))
    row_flip = (1 - 2 * row_bits).astype(f32)[:, None]
    col_flip = (1 - 2 * col_bits).astype(f32)
    high, low, twiddles = column_tables()
    tile = pl.pallas_call(
        project_kernel,
        out_shape=pltpu.VMEM((TILE_ROWS, BLOCK), bf16),
        in_specs=[IN_SMEM] + [IN_VMEM] * 4,
        out_specs=IN_VMEM,
        name="project",
    )(GROUP_ROWS * sides, near(rows_own), near(rows_other), near(right_cols), col_flip)
    partial_cols = pl.pallas_call(
        whiten_kernel,
        out_shape=pltpu.VMEM((ROWS, 2 * GROUP_ROWS, BLOCK), bf16),
        in_specs=[IN_SMEM] + [IN_VMEM] * 7,
        out_specs=IN_VMEM,
        scratch_shapes=[
            pltpu.VMEM((DM, BLOCK), f32),
            pltpu.VMEM((RADIX, 2 * INNER, BLOCK), f32),
        ],
        name="whiten",
    )((TILE_ROWS // NC) * sides, near(tile), near(left_own), near(left_other), row_flip, high, low, twiddles)
    partial_rows = lax.all_to_all(partial_cols, ROW_AXES, 0, 0, tiled=True)

    spectrum_rows = row_id * GROUP_ROWS + jnp.arange(GROUP_ROWS, dtype=jnp.int32)
    columns = jnp.arange(DM, dtype=jnp.int32).reshape(NYC, 1, BLOCK)
    phase = spectrum_rows[None, :, None] * columns
    angle = phase.astype(f32) * (2.0 * math.pi / (DM * DM))
    cross = jnp.stack([jnp.cos(angle), -jnp.sin(angle)]) * (1.0 / DM)
    local_ids = listed[0, 0, 0] - row_id * (GROUP_ROWS * NYC)
    lane_row = jnp.arange(NYC * GROUP_ROWS, dtype=jnp.int32)
    chosen = (
        (lane_row // GROUP_ROWS)[None, None, :] == jnp.arange(NYC, dtype=jnp.int32)[:, None, None]
    ) & ((lane_row % GROUP_ROWS)[None, None, :] == (local_ids // NYC)[None, :, None])
    chosen = chosen.reshape(NYC * list_len, NYC * GROUP_ROWS).astype(bf16)
    block_of = jnp.tile(local_ids % NYC, NYC)[:, None]
    source = jnp.arange(NYC * BLOCK, dtype=jnp.int32)
    target = NYC * (source % (BLOCK // NYC)) + source // BLOCK
    spread = (target[:, None] == jnp.arange(BLOCK, dtype=jnp.int32)[None, :]).astype(bf16)
    row_high, row_low, turns = row_tables()
    picked = pl.pallas_call(
        spectrum_kernel,
        out_shape=pltpu.VMEM((list_len, 2 * BLOCK), bf16),
        in_specs=[IN_VMEM] * 8,
        out_specs=IN_VMEM,
        scratch_shapes=[pltpu.VMEM((NYC, GROUP_ROWS, 2 * BLOCK), f32)],
        name="spectrum",
    )(near(partial_rows), near(cross), turns, row_high, row_low, near(chosen), block_of, near(spread))

    entries = lax.all_to_all(
        jnp.broadcast_to(picked[None], (NE,) + picked.shape), "e", 0, 0, tiled=True
    ).reshape(NE * list_len, 2 * BLOCK)
    owner_ids = owners[0, 0, :, :, 0].reshape(-1)
    order = jnp.arange(NE * list_len, dtype=jnp.int32)
    same = (owner_ids[:, None] == owner_ids[None, :]) & (order[:, None] < order[None, :])
    position = owner_ids * capacity + jnp.sum(same.astype(jnp.int32), axis=0)
    place = jnp.arange(ROWS * capacity, dtype=jnp.int32)[:, None] == position[None, :]
    outgoing = dot(place.astype(bf16), entries).astype(bf16)
    outgoing = outgoing.reshape(ROWS, capacity, 2 * BLOCK)
    arrived = lax.all_to_all(outgoing, ROW_AXES, 0, 0, tiled=True)
    return arrived.astype(f32)[None, None]


def solution(mesh):
    split = Mesh(mesh.devices.reshape(NZ, NY, NC, NE), ("z", "y", "c", "e"))
    in_specs = (
        P(None, "e", ROW_AXES, None),
        P(ROW_AXES, "e"),
        P(ROW_AXES + ("e",), None),
        P(),
        P(),
        P(None, ROW_AXES, "e", None),
        P(None, ROW_AXES, None, None, None),
    )
    out_specs = P(None, ROW_AXES, None, None, None)
    return jax.shard_map(shards, mesh=split, in_specs=in_specs, out_specs=out_specs, check_vma=False)
```

```python
import math

import jax
import jax.numpy as jnp
import numpy as np
from jax import lax
from jax.experimental import pallas as pl
from jax.experimental.pallas import tpu as pltpu
from jax.sharding import Mesh
from jax.sharding import PartitionSpec as P

DM = 2048
BLOCK = 128
NZ, NY, NC, NE = 8, 8, 2, 4
NYC = NY * NC
ROWS = NZ * NYC
GROUP_ROWS = DM // ROWS
TILE_ROWS = DM // NZ
RADIX = 8
INNER = DM // RADIX
ROOT_HALF = math.sqrt(0.5)

f32 = jnp.float32
bf16 = jnp.bfloat16
ROW_AXES = ("z", "y", "c")
IN_VMEM = pl.BlockSpec(memory_space=pltpu.VMEM)
IN_SMEM = pl.BlockSpec(memory_space=pltpu.SMEM)


def split_table(table):
    high = table.astype(bf16)
    low = (table - high.astype(np.float64)).astype(bf16)
    return high, low


def dft_angles(rows, cols, length):
    return 2.0 * math.pi * ((np.arange(rows)[:, None] * np.arange(cols)[None, :]) % length) / length


def column_tables():
    angles = dft_angles(INNER, INNER, INNER)
    high, low = split_table(np.concatenate([np.cos(angles), -np.sin(angles)], axis=0))
    angles = dft_angles(INNER, RADIX, DM)
    twiddles = np.concatenate([np.cos(angles), -np.sin(angles)], axis=1).astype(np.float32)
    return high, low, twiddles


def row_tables():
    angles = dft_angles(BLOCK, BLOCK, BLOCK)
    real, imag = np.cos(angles), -np.sin(angles)
    full = np.concatenate(
        [np.concatenate([real, imag], axis=1), np.concatenate([-imag, real], axis=1)], axis=0
    )
    high, low = split_table(full)
    angles = dft_angles(NYC, BLOCK, DM)
    twiddles = np.stack([np.cos(angles), -np.sin(angles)]).astype(np.float32)
    return high, low, twiddles.reshape(2, NYC, 1, BLOCK)


def add(a, b):
    return (a[0] + b[0], a[1] + b[1])


def sub(a, b):
    return (a[0] - b[0], a[1] - b[1])


def mul(a, b):
    return (a[0] * b[0] - a[1] * b[1], a[0] * b[1] + a[1] * b[0])


def minus_i(a):
    return (a[1], -a[0])


def fft4(a, b, c, d):
    even, odd = add(a, c), sub(a, c)
    even2, odd2 = add(b, d), minus_i(sub(b, d))
    return [add(even, even2), add(odd, odd2), sub(even, even2), sub(odd, odd2)]


def fft8(terms):
    even = fft4(terms[0], terms[2], terms[4], terms[6])
    odd = fft4(terms[1], terms[3], terms[5], terms[7])
    one = ((odd[1][0] + odd[1][1]) * ROOT_HALF, (odd[1][1] - odd[1][0]) * ROOT_HALF)
    three = ((odd[3][1] - odd[3][0]) * ROOT_HALF, (odd[3][0] + odd[3][1]) * -ROOT_HALF)
    turned = [odd[0], one, minus_i(odd[2]), three]
    return [add(e, o) for e, o in zip(even, turned)] + [sub(e, o) for e, o in zip(even, turned)]


def fft16(terms):
    inner = [fft4(*[terms[4 * a + b] for a in range(4)]) for b in range(4)]
    out = [None] * 16
    for first in range(4):
        column = []
        for b in range(4):
            turn = -2.0 * math.pi * b * first / 16
            value = inner[b][first]
            if b * first:
                cos, sin = math.cos(turn), math.sin(turn)
                value = (value[0] * cos - value[1] * sin, value[0] * sin + value[1] * cos)
            column.append(value)
        for second, value in enumerate(fft4(*column)):
            out[first + 4 * second] = value
    return out


def dot(a, b):
    return jnp.dot(a, b, preferred_element_type=f32)


def arrange_kernel(pieces, right, left):
    quarter = GROUP_ROWS // NE
    first = lax.broadcasted_iota(jnp.int32, (ROWS, 2 * quarter, BLOCK), 1) < quarter
    rights, lefts = [], []
    for e in range(0, NE, 2):
        even, odd = pieces[e].astype(f32), pieces[e + 1].astype(f32)
        rights.append(jnp.where(first, even, pltpu.roll(odd, quarter, axis=1)))
        lefts.append(jnp.where(first, pltpu.roll(even, quarter, axis=1), odd))
    right[...] = jnp.concatenate(rights, axis=1).astype(bf16)
    left[...] = jnp.concatenate(lefts, axis=1).astype(bf16)


def project_kernel(rows, right, col_flip, out):
    out[...] = (dot(rows[...], right[...].reshape(DM, BLOCK)) * col_flip[...]).astype(bf16)


def whiten_kernel(place, tile, own, other, row_flip, high, low, twiddles, out, white, stage):
    left = jnp.concatenate([own[...].reshape(DM, BLOCK), other[...].reshape(DM, BLOCK)], axis=1)
    half = TILE_ROWS // NC
    halves = [tile[pl.ds(pl.multiple_of(place[k], half), half), :] for k in range(NC)]
    white[...] = dot(left, jnp.concatenate(halves, axis=0)) * row_flip[...]
    for p in range(RADIX):
        part = white[pl.ds(p, INNER, stride=RADIX), :]
        part_high = part.astype(bf16)
        part_low = (part - part_high.astype(f32)).astype(bf16)
        stage[p] = dot(high[...], part_high) + dot(low[...], part_high) + dot(high[...], part_low)

    def combine(step, carry):
        rows = pl.ds(pl.multiple_of(step * GROUP_ROWS, GROUP_ROWS), GROUP_ROWS)
        rows_imag = pl.ds(pl.multiple_of(INNER + step * GROUP_ROWS, GROUP_ROWS), GROUP_ROWS)
        factors = twiddles[rows, :]
        terms = [(stage[0, rows, :], stage[0, rows_imag, :])]
        for p in range(1, RADIX):
            factor = (factors[:, p : p + 1], factors[:, RADIX + p : RADIX + p + 1])
            terms.append(mul((stage[p, rows, :], stage[p, rows_imag, :]), factor))
        for k, value in enumerate(fft8(terms)):
            out[NYC * k + step, 0:GROUP_ROWS, :] = value[0].astype(bf16)
            out[NYC * k + step, GROUP_ROWS : 2 * GROUP_ROWS, :] = value[1].astype(bf16)
        return carry

    lax.fori_loop(0, INNER // GROUP_ROWS, combine, 0)


def spectrum_kernel(parts, cross, turns, high, low, chosen, block_of, spread, out, mixed):
    terms = []
    for yc in range(NYC):
        total = parts[yc].astype(f32)
        for z in range(1, NZ):
            total = total + parts[z * NYC + yc].astype(f32)
        terms.append(
            mul((total[0:GROUP_ROWS], total[GROUP_ROWS:]), (cross[0, yc], cross[1, yc]))
        )
    for k, value in enumerate(fft16(terms)):
        value = mul(value, (turns[0, k], turns[1, k]))
        mixed[k, :, 0:BLOCK] = value[0]
        mixed[k, :, BLOCK : 2 * BLOCK] = value[1]
    rows = mixed[...].reshape(NYC * GROUP_ROWS, 2 * BLOCK)
    rows_high = rows.astype(bf16)
    rows_low = (rows - rows_high.astype(f32)).astype(bf16)
    result = dot(rows_high, high[...]) + dot(rows_low, high[...]) + dot(rows_high, low[...])
    picked = dot(chosen[...], result.astype(bf16))
    count = picked.shape[0] // NYC
    lane_block = lax.broadcasted_iota(jnp.int32, (NYC * count, BLOCK), 1) // (BLOCK // NYC)
    keep = lane_block == block_of[...]
    sides = []
    for side in range(2):
        own = jnp.where(keep, picked[:, side * BLOCK : (side + 1) * BLOCK], 0.0).astype(bf16)
        own = own.reshape(NYC, count, BLOCK)
        wide = jnp.concatenate([own[k] for k in range(NYC)], axis=1)
        sides.append(dot(wide, spread[...]))
    out[...] = jnp.concatenate(sides, axis=1).astype(bf16)


def grant(mebibytes):
    return pltpu.CompilerParams(vmem_limit_bytes=mebibytes * 2**20)


def near(array):
    return pltpu.with_memory_space_constraint(array, pltpu.VMEM)


def shards(grads, right_inv, left_inv, row_signs, col_signs, listed, owners):
    z_id, y_id, c_id, e_id = (lax.axis_index(name) for name in ("z", "y", "c", "e"))
    yc_id = y_id * NC + c_id
    row_id = z_id * NYC + yc_id
    list_len = listed.shape[3]
    capacity = 2

    quarter = GROUP_ROWS // NE
    right_rows = right_inv.reshape(NE, quarter, NE, BLOCK).transpose(0, 2, 1, 3)
    right_rows = lax.all_to_all(right_rows, "e", 0, 0, tiled=True)
    right_rows = right_rows.reshape(1, NY, NC, quarter, BLOCK)
    left_rows = left_inv.reshape(quarter, NYC, BLOCK).transpose(1, 0, 2)
    left_rows = left_rows.reshape(NZ, 1, NC, quarter, BLOCK)
    whole = (NZ, NY, NC, quarter, BLOCK)
    pieces = jnp.concatenate(
        [jnp.broadcast_to(right_rows, whole), jnp.broadcast_to(left_rows, whole)], axis=3
    ).reshape(ROWS, 2 * quarter, BLOCK)
    pieces = lax.all_to_all(pieces, ROW_AXES, 0, 0, tiled=True)
    pieces = lax.all_to_all(jnp.broadcast_to(pieces[None], (NE,) + pieces.shape), "e", 0, 0, tiled=True)

    rows = lax.all_gather(grads.reshape(GROUP_ROWS, DM), ("y", "c"), axis=0, tiled=True)
    swap = [(0, 1), (1, 0)]
    factor_shape = pltpu.VMEM((ROWS, GROUP_ROWS, BLOCK), bf16)
    right_cols, left_own = pl.pallas_call(
        arrange_kernel,
        out_shape=(factor_shape, factor_shape),
        in_specs=[IN_VMEM],
        out_specs=(IN_VMEM, IN_VMEM),
        compiler_params=grant(12),
        name="arrange",
    )(near(pieces))
    left_other = lax.ppermute(left_own, "c", swap)
    sides = jnp.stack([c_id, 1 - c_id])

    row_bits = lax.dynamic_index_in_dim(row_signs[0], e_id, 0, keepdims=False)
    col_bits = lax.dynamic_slice(col_signs[0], (e_id, yc_id * BLOCK), (1, BLOCK))
    row_flip = (1 - 2 * row_bits).astype(f32)[:, None]
    col_flip = (1 - 2 * col_bits).astype(f32)
    high, low, twiddles = column_tables()
    tile = pl.pallas_call(
        project_kernel,
        out_shape=pltpu.VMEM((TILE_ROWS, BLOCK), bf16),
        in_specs=[IN_VMEM] * 3,
        out_specs=IN_VMEM,
        compiler_params=grant(6),
        name="project",
    )(rows, near(right_cols), col_flip)
    partial_cols = pl.pallas_call(
        whiten_kernel,
        out_shape=pltpu.VMEM((ROWS, 2 * GROUP_ROWS, BLOCK), bf16),
        in_specs=[IN_SMEM] + [IN_VMEM] * 7,
        out_specs=IN_VMEM,
        scratch_shapes=[
            pltpu.VMEM((DM, BLOCK), f32),
            pltpu.VMEM((RADIX, 2 * INNER, BLOCK), f32),
        ],
        compiler_params=grant(16),
        name="whiten",
    )((TILE_ROWS // NC) * sides, near(tile), near(left_own), near(left_other), row_flip, high, low, twiddles)
    partial_rows = lax.all_to_all(partial_cols, ROW_AXES, 0, 0, tiled=True)

    spectrum_rows = row_id * GROUP_ROWS + jnp.arange(GROUP_ROWS, dtype=jnp.int32)
    columns = jnp.arange(DM, dtype=jnp.int32).reshape(NYC, 1, BLOCK)
    phase = spectrum_rows[None, :, None] * columns
    angle = phase.astype(f32) * (2.0 * math.pi / (DM * DM))
    cross = jnp.stack([jnp.cos(angle), -jnp.sin(angle)]) * (1.0 / DM)
    local_ids = listed[0, 0, 0] - row_id * (GROUP_ROWS * NYC)
    lane_row = jnp.arange(NYC * GROUP_ROWS, dtype=jnp.int32)
    chosen = (
        (lane_row // GROUP_ROWS)[None, None, :] == jnp.arange(NYC, dtype=jnp.int32)[:, None, None]
    ) & ((lane_row % GROUP_ROWS)[None, None, :] == (local_ids // NYC)[None, :, None])
    chosen = chosen.reshape(NYC * list_len, NYC * GROUP_ROWS).astype(bf16)
    block_of = jnp.tile(local_ids % NYC, NYC)[:, None]
    source = jnp.arange(NYC * BLOCK, dtype=jnp.int32)
    target = NYC * (source % (BLOCK // NYC)) + source // BLOCK
    spread = (target[:, None] == jnp.arange(BLOCK, dtype=jnp.int32)[None, :]).astype(bf16)
    row_high, row_low, turns = row_tables()
    picked = pl.pallas_call(
        spectrum_kernel,
        out_shape=pltpu.VMEM((list_len, 2 * BLOCK), bf16),
        in_specs=[IN_VMEM] * 8,
        out_specs=IN_VMEM,
        scratch_shapes=[pltpu.VMEM((NYC, GROUP_ROWS, 2 * BLOCK), f32)],
        compiler_params=grant(12),
        name="spectrum",
    )(near(partial_rows), near(cross), turns, row_high, row_low, near(chosen), block_of, near(spread))

    entries = lax.all_to_all(
        jnp.broadcast_to(picked[None], (NE,) + picked.shape), "e", 0, 0, tiled=True
    ).reshape(NE * list_len, 2 * BLOCK)
    owner_ids = owners[0, 0, :, :, 0].reshape(-1)
    order = jnp.arange(NE * list_len, dtype=jnp.int32)
    same = (owner_ids[:, None] == owner_ids[None, :]) & (order[:, None] < order[None, :])
    position = owner_ids * capacity + jnp.sum(same.astype(jnp.int32), axis=0)
    place = jnp.arange(ROWS * capacity, dtype=jnp.int32)[:, None] == position[None, :]
    outgoing = dot(place.astype(bf16), entries).astype(bf16)
    outgoing = outgoing.reshape(ROWS, capacity, 2 * BLOCK)
    arrived = lax.all_to_all(outgoing, ROW_AXES, 0, 0, tiled=True)
    return arrived.astype(f32)[None, None]


def solution(mesh):
    split = Mesh(mesh.devices.reshape(NZ, NY, NC, NE), ("z", "y", "c", "e"))
    in_specs = (
        P(None, "e", ROW_AXES, None),
        P(ROW_AXES, "e"),
        P(ROW_AXES + ("e",), None),
        P(),
        P(),
        P(None, ROW_AXES, "e", None),
        P(None, ROW_AXES, None, None, None),
    )
    out_specs = P(None, ROW_AXES, None, None, None)
    return jax.shard_map(shards, mesh=split, in_specs=in_specs, out_specs=out_specs, check_vma=False)
```

```python
import math

import jax
import jax.numpy as jnp
import numpy as np
from jax import lax
from jax.experimental import pallas as pl
from jax.experimental.pallas import tpu as pltpu
from jax.sharding import Mesh
from jax.sharding import PartitionSpec as P

DM = 2048
BLOCK = 128
NZ, NY, NC, NE = 8, 8, 2, 4
NYC = NY * NC
ROWS = NZ * NYC
GROUP_ROWS = DM // ROWS
TILE_ROWS = DM // NZ
RADIX = 8
INNER = DM // RADIX
ROOT_HALF = math.sqrt(0.5)

f32 = jnp.float32
bf16 = jnp.bfloat16
ROW_AXES = ("z", "y", "c")
IN_VMEM = pl.BlockSpec(memory_space=pltpu.VMEM)
IN_SMEM = pl.BlockSpec(memory_space=pltpu.SMEM)


def split_table(table):
    high = table.astype(bf16)
    low = (table - high.astype(np.float64)).astype(bf16)
    return high, low


def dft_angles(rows, cols, length):
    return 2.0 * math.pi * ((np.arange(rows)[:, None] * np.arange(cols)[None, :]) % length) / length


def column_tables():
    angles = dft_angles(INNER, INNER, INNER)
    high, low = split_table(np.concatenate([np.cos(angles), -np.sin(angles)], axis=0))
    angles = dft_angles(INNER, RADIX, DM)
    twiddles = np.concatenate([np.cos(angles), -np.sin(angles)], axis=1).astype(np.float32)
    return high, low, twiddles


def row_tables():
    angles = dft_angles(BLOCK, BLOCK, BLOCK)
    real, imag = np.cos(angles), -np.sin(angles)
    full = np.concatenate(
        [np.concatenate([real, imag], axis=1), np.concatenate([-imag, real], axis=1)], axis=0
    )
    high, low = split_table(full)
    angles = dft_angles(NYC, BLOCK, DM)
    twiddles = np.stack([np.cos(angles), -np.sin(angles)]).astype(np.float32)
    return high, low, twiddles.reshape(2, NYC, 1, BLOCK)


def add(a, b):
    return (a[0] + b[0], a[1] + b[1])


def sub(a, b):
    return (a[0] - b[0], a[1] - b[1])


def mul(a, b):
    return (a[0] * b[0] - a[1] * b[1], a[0] * b[1] + a[1] * b[0])


def minus_i(a):
    return (a[1], -a[0])


def fft4(a, b, c, d):
    even, odd = add(a, c), sub(a, c)
    even2, odd2 = add(b, d), minus_i(sub(b, d))
    return [add(even, even2), add(odd, odd2), sub(even, even2), sub(odd, odd2)]


def fft8(terms):
    even = fft4(terms[0], terms[2], terms[4], terms[6])
    odd = fft4(terms[1], terms[3], terms[5], terms[7])
    one = ((odd[1][0] + odd[1][1]) * ROOT_HALF, (odd[1][1] - odd[1][0]) * ROOT_HALF)
    three = ((odd[3][1] - odd[3][0]) * ROOT_HALF, (odd[3][0] + odd[3][1]) * -ROOT_HALF)
    turned = [odd[0], one, minus_i(odd[2]), three]
    return [add(e, o) for e, o in zip(even, turned)] + [sub(e, o) for e, o in zip(even, turned)]


def fft16(terms):
    inner = [fft4(*[terms[4 * a + b] for a in range(4)]) for b in range(4)]
    out = [None] * 16
    for first in range(4):
        column = []
        for b in range(4):
            turn = -2.0 * math.pi * b * first / 16
            value = inner[b][first]
            if b * first:
                cos, sin = math.cos(turn), math.sin(turn)
                value = (value[0] * cos - value[1] * sin, value[0] * sin + value[1] * cos)
            column.append(value)
        for second, value in enumerate(fft4(*column)):
            out[first + 4 * second] = value
    return out


def dot(a, b):
    return jnp.dot(a, b, preferred_element_type=f32)


def deal_kernel(right, left, out):
    quarter = GROUP_ROWS // NE
    width = right.shape[1]
    pack = BLOCK // NE
    column = lax.broadcasted_iota(jnp.int32, (width, width), 0)
    target = lax.broadcasted_iota(jnp.int32, (width, width), 1)
    order = target == pack * (column % NYC) + column // NYC
    sorted_cols = dot(right[...], jnp.where(order, 1.0, 0.0).astype(bf16))
    tail = left[...].astype(f32)
    tail = jnp.concatenate([tail, tail], axis=0)
    shape = (2 * quarter, BLOCK)
    upper = lax.broadcasted_iota(jnp.int32, shape, 0) < quarter
    lane_group = lax.broadcasted_iota(jnp.int32, shape, 1) // pack
    for tile in range(width // BLOCK):
        lanes = slice(tile * BLOCK, (tile + 1) * BLOCK)
        row_groups = []
        for half in range(2):
            value = sorted_cols[2 * quarter * half : 2 * quarter * (half + 1), lanes]
            row_groups += [value, pltpu.roll(value, quarter, axis=0)]
        for group in range(NE):
            yc = tile * NE + group
            piece = None
            for p in range(NE):
                moved = row_groups[p]
                if p != group:
                    moved = pltpu.roll(moved, (pack * (p - group)) % BLOCK, axis=1)
                piece = moved if piece is None else jnp.where(lane_group == p, moved, piece)
            for z in range(NZ):
                zc = z * NC + yc % NC
                both = jnp.where(upper, piece, tail[:, zc * BLOCK : (zc + 1) * BLOCK])
                out[z * NYC + yc] = both.astype(bf16)


def arrange_kernel(pieces, right, left):
    quarter = GROUP_ROWS // NE
    pack = BLOCK // NE
    shape = (ROWS, 2 * quarter, BLOCK)
    first = lax.broadcasted_iota(jnp.int32, shape, 1) < quarter
    lane_group = lax.broadcasted_iota(jnp.int32, shape, 2) // pack
    values = [pieces[e].astype(f32) for e in range(NE)]
    unpacked = []
    for p in range(NE):
        rows = None
        for e in range(NE):
            moved = values[e]
            if e != p:
                moved = pltpu.roll(moved, (pack * (e - p)) % BLOCK, axis=2)
            rows = moved if rows is None else jnp.where(lane_group == e, moved, rows)
        unpacked.append(rows)
    rights, lefts = [], []
    for e in range(0, NE, 2):
        rights.append(jnp.where(first, unpacked[e], pltpu.roll(unpacked[e + 1], quarter, axis=1)))
        lefts.append(jnp.where(first, pltpu.roll(values[e], quarter, axis=1), values[e + 1]))
    right[...] = jnp.concatenate(rights, axis=1).astype(bf16)
    left[...] = jnp.concatenate(lefts, axis=1).astype(bf16)


def project_kernel(rows, right, col_flip, out):
    out[...] = (dot(rows[...], right[...].reshape(DM, BLOCK)) * col_flip[...]).astype(bf16)


def whiten_kernel(place, tile, own, other, row_flip, high, low, twiddles, out, white, stage):
    left = jnp.concatenate([own[...].reshape(DM, BLOCK), other[...].reshape(DM, BLOCK)], axis=1)
    half = TILE_ROWS // NC
    halves = [tile[pl.ds(pl.multiple_of(place[k], half), half), :] for k in range(NC)]
    white[...] = dot(left, jnp.concatenate(halves, axis=0)) * row_flip[...]
    for p in range(RADIX):
        part = white[pl.ds(p, INNER, stride=RADIX), :]
        part_high = part.astype(bf16)
        part_low = (part - part_high.astype(f32)).astype(bf16)
        stage[p] = dot(high[...], part_high) + dot(low[...], part_high) + dot(high[...], part_low)

    def combine(step, carry):
        rows = pl.ds(pl.multiple_of(step * GROUP_ROWS, GROUP_ROWS), GROUP_ROWS)
        rows_imag = pl.ds(pl.multiple_of(INNER + step * GROUP_ROWS, GROUP_ROWS), GROUP_ROWS)
        factors = twiddles[rows, :]
        terms = [(stage[0, rows, :], stage[0, rows_imag, :])]
        for p in range(1, RADIX):
            factor = (factors[:, p : p + 1], factors[:, RADIX + p : RADIX + p + 1])
            terms.append(mul((stage[p, rows, :], stage[p, rows_imag, :]), factor))
        for k, value in enumerate(fft8(terms)):
            out[NYC * k + step, 0:GROUP_ROWS, :] = value[0].astype(bf16)
            out[NYC * k + step, GROUP_ROWS : 2 * GROUP_ROWS, :] = value[1].astype(bf16)
        return carry

    lax.fori_loop(0, INNER // GROUP_ROWS, combine, 0)


def spectrum_kernel(parts, cross, turns, high, low, wanted, out, mixed):
    for yc in range(NYC):
        total = parts[yc].astype(f32)
        for z in range(1, NZ):
            total = total + parts[z * NYC + yc].astype(f32)
        value = mul((total[0:GROUP_ROWS], total[GROUP_ROWS:]), (cross[0, yc], cross[1, yc]))
        mixed[yc, :, 0:BLOCK] = value[0]
        mixed[yc, :, BLOCK : 2 * BLOCK] = value[1]
    rows = mixed[...].reshape(NYC * GROUP_ROWS, 2 * BLOCK)
    rows_high = rows.astype(bf16)
    rows_low = (rows - rows_high.astype(f32)).astype(bf16)
    rows = dot(rows_high, high[...]) + dot(rows_low, high[...]) + dot(rows_high, low[...])
    rows = rows.reshape(NYC, GROUP_ROWS, 2 * BLOCK)
    terms = [
        mul((rows[yc, :, 0:BLOCK], rows[yc, :, BLOCK:]), (turns[0, yc], turns[1, yc]))
        for yc in range(NYC)
    ]
    blocks = [jnp.concatenate(value, axis=1).astype(bf16) for value in fft16(terms)]
    blocks = jnp.concatenate(blocks, axis=0)
    row = lax.broadcasted_iota(jnp.int32, (out.shape[0], NYC * GROUP_ROWS), 1)
    chosen = jnp.where(row == wanted[...], 1.0, 0.0).astype(bf16)
    out[...] = dot(chosen, blocks).astype(bf16)


def grant(mebibytes):
    return pltpu.CompilerParams(vmem_limit_bytes=mebibytes * 2**20)


def near(array):
    return pltpu.with_memory_space_constraint(array, pltpu.VMEM)


def shards(grads, right_inv, left_inv, row_signs, col_signs, listed, owners):
    z_id, y_id, c_id, e_id = (lax.axis_index(name) for name in ("z", "y", "c", "e"))
    yc_id = y_id * NC + c_id
    row_id = z_id * NYC + yc_id
    list_len = listed.shape[3]
    capacity = 2

    pieces = pl.pallas_call(
        deal_kernel,
        out_shape=pltpu.VMEM((ROWS, 2 * GROUP_ROWS // NE, BLOCK), bf16),
        in_specs=[IN_VMEM] * 2,
        out_specs=IN_VMEM,
        compiler_params=grant(8),
        name="deal",
    )(right_inv, left_inv)
    pieces = lax.all_to_all(pieces, ROW_AXES, 0, 0, tiled=True)
    pieces = lax.all_to_all(jnp.broadcast_to(pieces[None], (NE,) + pieces.shape), "e", 0, 0, tiled=True)

    rows = lax.all_gather(grads.reshape(GROUP_ROWS, DM), ("y", "c"), axis=0, tiled=True)
    swap = [(0, 1), (1, 0)]
    factor_shape = pltpu.VMEM((ROWS, GROUP_ROWS, BLOCK), bf16)
    right_cols, left_own = pl.pallas_call(
        arrange_kernel,
        out_shape=(factor_shape, factor_shape),
        in_specs=[IN_VMEM],
        out_specs=(IN_VMEM, IN_VMEM),
        compiler_params=grant(12),
        name="arrange",
    )(near(pieces))
    left_other = lax.ppermute(left_own, "c", swap)
    sides = jnp.stack([c_id, 1 - c_id])

    row_bits = lax.dynamic_index_in_dim(row_signs[0], e_id, 0, keepdims=False)
    col_bits = lax.dynamic_index_in_dim(col_signs[0], e_id, 0, keepdims=False)
    col_bits = col_bits.reshape(BLOCK, NYC)
    own_col = jnp.arange(NYC, dtype=jnp.int32) == yc_id
    col_bits = jnp.sum(jnp.where(own_col[None, :], col_bits, 0), axis=1)[None, :]
    row_flip = (1 - 2 * row_bits).astype(f32)[:, None]
    col_flip = (1 - 2 * col_bits).astype(f32)
    high, low, twiddles = column_tables()
    tile = pl.pallas_call(
        project_kernel,
        out_shape=pltpu.VMEM((TILE_ROWS, BLOCK), bf16),
        in_specs=[IN_VMEM] * 3,
        out_specs=IN_VMEM,
        compiler_params=grant(6),
        name="project",
    )(rows, near(right_cols), col_flip)
    partial_cols = pl.pallas_call(
        whiten_kernel,
        out_shape=pltpu.VMEM((ROWS, 2 * GROUP_ROWS, BLOCK), bf16),
        in_specs=[IN_SMEM] + [IN_VMEM] * 7,
        out_specs=IN_VMEM,
        scratch_shapes=[
            pltpu.VMEM((DM, BLOCK), f32),
            pltpu.VMEM((RADIX, 2 * INNER, BLOCK), f32),
        ],
        compiler_params=grant(16),
        name="whiten",
    )((TILE_ROWS // NC) * sides, near(tile), near(left_own), near(left_other), row_flip, high, low, twiddles)
    partial_rows = lax.all_to_all(partial_cols, ROW_AXES, 0, 0, tiled=True)

    spectrum_rows = row_id * GROUP_ROWS + jnp.arange(GROUP_ROWS, dtype=jnp.int32)
    columns = jnp.arange(NYC, dtype=jnp.int32)[:, None] + NYC * jnp.arange(BLOCK, dtype=jnp.int32)
    columns = columns.reshape(NYC, 1, BLOCK)
    phase = spectrum_rows[None, :, None] * columns
    angle = phase.astype(f32) * (2.0 * math.pi / (DM * DM))
    cross = jnp.stack([jnp.cos(angle), -jnp.sin(angle)]) * (1.0 / DM)
    local_ids = listed[0, 0, 0] - row_id * (GROUP_ROWS * NYC)
    wanted = (local_ids % NYC) * GROUP_ROWS + local_ids // NYC
    row_high, row_low, turns = row_tables()
    picked = pl.pallas_call(
        spectrum_kernel,
        out_shape=pltpu.VMEM((list_len, 2 * BLOCK), bf16),
        in_specs=[IN_VMEM] * 6,
        out_specs=IN_VMEM,
        scratch_shapes=[pltpu.VMEM((NYC, GROUP_ROWS, 2 * BLOCK), f32)],
        compiler_params=grant(12),
        name="spectrum",
    )(near(partial_rows), near(cross), turns, row_high, row_low, wanted[:, None])

    entries = lax.all_to_all(
        jnp.broadcast_to(picked[None], (NE,) + picked.shape), "e", 0, 0, tiled=True
    ).reshape(NE * list_len, 2 * BLOCK)
    owner_ids = owners[0, 0, :, :, 0].reshape(-1)
    order = jnp.arange(NE * list_len, dtype=jnp.int32)
    same = (owner_ids[:, None] == owner_ids[None, :]) & (order[:, None] < order[None, :])
    position = owner_ids * capacity + jnp.sum(same.astype(jnp.int32), axis=0)
    place = jnp.arange(ROWS * capacity, dtype=jnp.int32)[:, None] == position[None, :]
    outgoing = dot(place.astype(bf16), entries).astype(bf16)
    outgoing = outgoing.reshape(ROWS, capacity, 2 * BLOCK)
    arrived = lax.all_to_all(outgoing, ROW_AXES, 0, 0, tiled=True)
    return arrived.astype(f32)[None, None]


def solution(mesh):
    split = Mesh(mesh.devices.reshape(NZ, NY, NC, NE), ("z", "y", "c", "e"))
    in_specs = (
        P(None, "e", ROW_AXES, None),
        P(ROW_AXES, "e"),
        P(ROW_AXES + ("e",), None),
        P(),
        P(),
        P(None, ROW_AXES, "e", None),
        P(None, ROW_AXES, None, None, None),
    )
    out_specs = P(None, ROW_AXES, None, None, None)
    return jax.shard_map(shards, mesh=split, in_specs=in_specs, out_specs=out_specs, check_vma=False)
```

```python
import math

import jax
import jax.numpy as jnp
import numpy as np
from jax import lax
from jax.experimental import pallas as pl
from jax.experimental.pallas import tpu as pltpu
from jax.sharding import Mesh
from jax.sharding import PartitionSpec as P


DM = 2048
BLOCK = 128
NZ, NY, NC, NE = 8, 8, 2, 4
NYC = NY * NC
ROWS = NZ * NYC
GROUP_ROWS = DM // ROWS
TILE_ROWS = DM // NZ
RADIX = 8
INNER = DM // RADIX
ROOT_HALF = math.sqrt(0.5)

f32 = jnp.float32
bf16 = jnp.bfloat16
ROW_AXES = ("z", "y", "c")
IN_VMEM = pl.BlockSpec(memory_space=pltpu.VMEM)
IN_SMEM = pl.BlockSpec(memory_space=pltpu.SMEM)


def split_table(table):
    high = table.astype(bf16)
    low = (table - high.astype(np.float64)).astype(bf16)
    return high, low


def dft_angles(rows, cols, length):
    return 2.0 * math.pi * ((np.arange(rows)[:, None] * np.arange(cols)[None, :]) % length) / length


def column_tables():
    angles = dft_angles(INNER, INNER, INNER)
    high, low = split_table(np.concatenate([np.cos(angles), -np.sin(angles)], axis=0))
    angles = dft_angles(INNER, RADIX, DM)
    twiddles = np.concatenate([np.cos(angles), -np.sin(angles)], axis=1).astype(np.float32)
    return high, low, twiddles


def row_tables():
    angles = dft_angles(BLOCK, BLOCK, BLOCK)
    real, imag = np.cos(angles), -np.sin(angles)
    full = np.concatenate(
        [np.concatenate([real, imag], axis=1), np.concatenate([-imag, real], axis=1)], axis=0
    )
    high, low = split_table(full)
    angles = dft_angles(NYC, BLOCK, DM)
    twiddles = np.stack([np.cos(angles), -np.sin(angles)]).astype(np.float32)
    return high, low, twiddles.reshape(2, NYC, 1, BLOCK)


def add(a, b):
    return (a[0] + b[0], a[1] + b[1])


def sub(a, b):
    return (a[0] - b[0], a[1] - b[1])


def mul(a, b):
    return (a[0] * b[0] - a[1] * b[1], a[0] * b[1] + a[1] * b[0])


def minus_i(a):
    return (a[1], -a[0])


def fft4(a, b, c, d):
    even, odd = add(a, c), sub(a, c)
    even2, odd2 = add(b, d), minus_i(sub(b, d))
    return [add(even, even2), add(odd, odd2), sub(even, even2), sub(odd, odd2)]


def fft8(terms):
    even = fft4(terms[0], terms[2], terms[4], terms[6])
    odd = fft4(terms[1], terms[3], terms[5], terms[7])
    one = ((odd[1][0] + odd[1][1]) * ROOT_HALF, (odd[1][1] - odd[1][0]) * ROOT_HALF)
    three = ((odd[3][1] - odd[3][0]) * ROOT_HALF, (odd[3][0] + odd[3][1]) * -ROOT_HALF)
    turned = [odd[0], one, minus_i(odd[2]), three]
    return [add(e, o) for e, o in zip(even, turned)] + [sub(e, o) for e, o in zip(even, turned)]


def fft16(terms):
    inner = [fft4(*[terms[4 * a + b] for a in range(4)]) for b in range(4)]
    out = [None] * 16
    for first in range(4):
        column = []
        for b in range(4):
            turn = -2.0 * math.pi * b * first / 16
            value = inner[b][first]
            if b * first:
                cos, sin = math.cos(turn), math.sin(turn)
                value = (value[0] * cos - value[1] * sin, value[0] * sin + value[1] * cos)
            column.append(value)
        for second, value in enumerate(fft4(*column)):
            out[first + 4 * second] = value
    return out


def dot(a, b):
    return jnp.dot(a, b, preferred_element_type=f32)


def deal_kernel(right, left, out):
    quarter = GROUP_ROWS // NE
    width = right.shape[1]
    pack = BLOCK // NE
    column = lax.broadcasted_iota(jnp.int32, (width, width), 0)
    target = lax.broadcasted_iota(jnp.int32, (width, width), 1)
    order = target == pack * (column % NYC) + column // NYC
    sorted_cols = dot(right[...], jnp.where(order, 1.0, 0.0).astype(bf16))
    tail = left[...].astype(f32)
    tail = jnp.concatenate([tail, tail], axis=0)
    shape = (2 * quarter, BLOCK)
    upper = lax.broadcasted_iota(jnp.int32, shape, 0) < quarter
    lane_group = lax.broadcasted_iota(jnp.int32, shape, 1) // pack
    for tile in range(width // BLOCK):
        lanes = slice(tile * BLOCK, (tile + 1) * BLOCK)
        row_groups = []
        for half in range(2):
            value = sorted_cols[2 * quarter * half : 2 * quarter * (half + 1), lanes]
            row_groups += [value, pltpu.roll(value, quarter, axis=0)]
        for group in range(NE):
            yc = tile * NE + group
            piece = None
            for p in range(NE):
                moved = row_groups[p]
                if p != group:
                    moved = pltpu.roll(moved, (pack * (p - group)) % BLOCK, axis=1)
                piece = moved if piece is None else jnp.where(lane_group == p, moved, piece)
            for z in range(NZ):
                zc = z * NC + yc % NC
                both = jnp.where(upper, piece, tail[:, zc * BLOCK : (zc + 1) * BLOCK])
                out[z * NYC + yc] = both.astype(bf16)


def arrange_kernel(pieces, right, left):
    quarter = GROUP_ROWS // NE
    pack = BLOCK // NE
    shape = (ROWS, 2 * quarter, BLOCK)
    first = lax.broadcasted_iota(jnp.int32, shape, 1) < quarter
    lane_group = lax.broadcasted_iota(jnp.int32, shape, 2) // pack
    values = [pieces[e].astype(f32) for e in range(NE)]
    unpacked = []
    for p in range(NE):
        rows = None
        for e in range(NE):
            moved = values[e]
            if e != p:
                moved = pltpu.roll(moved, (pack * (e - p)) % BLOCK, axis=2)
            rows = moved if rows is None else jnp.where(lane_group == e, moved, rows)
        unpacked.append(rows)
    rights, lefts = [], []
    for e in range(0, NE, 2):
        rights.append(jnp.where(first, unpacked[e], pltpu.roll(unpacked[e + 1], quarter, axis=1)))
        lefts.append(jnp.where(first, pltpu.roll(values[e], quarter, axis=1), values[e + 1]))
    right[...] = jnp.concatenate(rights, axis=1).astype(bf16)
    left[...] = jnp.concatenate(lefts, axis=1).astype(bf16)


def project_kernel(place, own, other, right, col_flip, out):
    factor = right[...].reshape(DM, BLOCK)
    for side, rows in enumerate((own, other)):
        part = dot(rows[...].reshape(TILE_ROWS // NC, DM), factor) * col_flip[...]
        part = part.astype(bf16).reshape(NY, GROUP_ROWS, BLOCK)
        for k in range(NY):
            from_y = (place[0] + NY // 2 + k) % NY
            from_c = place[1] if side == 0 else 1 - place[1]
            start = pl.multiple_of(GROUP_ROWS * (NC * from_y + from_c), GROUP_ROWS)
            out[pl.ds(start, GROUP_ROWS), :] = part[k]


def whiten_kernel(place, tile, own, other, row_flip, high, low, twiddles, out, white, stage):
    left = jnp.concatenate([own[...].reshape(DM, BLOCK), other[...].reshape(DM, BLOCK)], axis=1)
    half = TILE_ROWS // NC
    starts = [pl.multiple_of(half * side, half) for side in (place[1], 1 - place[1])]
    halves = [tile[pl.ds(start, half), :] for start in starts]
    white[...] = dot(left, jnp.concatenate(halves, axis=0)) * row_flip[...]
    for p in range(0, RADIX, 2):
        pair = [white[pl.ds(p + k, INNER, stride=RADIX), :] for k in range(2)]
        part = jnp.concatenate(pair, axis=1)
        part_high = part.astype(bf16)
        part_low = (part - part_high.astype(f32)).astype(bf16)
        both = dot(high[...], part_high) + dot(low[...], part_high) + dot(high[...], part_low)
        stage[p] = both[:, 0:BLOCK]
        stage[p + 1] = both[:, BLOCK:]

    def combine(step, carry):
        rows = pl.ds(pl.multiple_of(step * GROUP_ROWS, GROUP_ROWS), GROUP_ROWS)
        rows_imag = pl.ds(pl.multiple_of(INNER + step * GROUP_ROWS, GROUP_ROWS), GROUP_ROWS)
        factors = twiddles[rows, :]
        terms = [(stage[0, rows, :], stage[0, rows_imag, :])]
        for p in range(1, RADIX):
            factor = (factors[:, p : p + 1], factors[:, RADIX + p : RADIX + p + 1])
            terms.append(mul((stage[p, rows, :], stage[p, rows_imag, :]), factor))
        for k, value in enumerate(fft8(terms)):
            out[NYC * k + step, 0:GROUP_ROWS, :] = value[0].astype(bf16)
            out[NYC * k + step, GROUP_ROWS : 2 * GROUP_ROWS, :] = value[1].astype(bf16)
        return carry

    lax.fori_loop(0, INNER // GROUP_ROWS, combine, 0, unroll=4)


def spectrum_kernel(parts, cross, turns, high, low, wanted, out, mixed):
    for yc in range(NYC):
        total = parts[yc].astype(f32)
        for z in range(1, NZ):
            total = total + parts[z * NYC + yc].astype(f32)
        value = mul((total[0:GROUP_ROWS], total[GROUP_ROWS:]), (cross[0, yc], cross[1, yc]))
        mixed[yc, :, 0:BLOCK] = value[0]
        mixed[yc, :, BLOCK : 2 * BLOCK] = value[1]
    rows = mixed[...].reshape(NYC * GROUP_ROWS, 2 * BLOCK)
    rows_high = rows.astype(bf16)
    rows_low = (rows - rows_high.astype(f32)).astype(bf16)
    rows = dot(rows_high, high[...]) + dot(rows_low, high[...]) + dot(rows_high, low[...])
    rows = rows.reshape(NYC, GROUP_ROWS, 2 * BLOCK)
    terms = [
        mul((rows[yc, :, 0:BLOCK], rows[yc, :, BLOCK:]), (turns[0, yc], turns[1, yc]))
        for yc in range(NYC)
    ]
    blocks = [jnp.concatenate(value, axis=1).astype(bf16) for value in fft16(terms)]
    blocks = jnp.concatenate(blocks, axis=0)
    row = lax.broadcasted_iota(jnp.int32, (out.shape[0], NYC * GROUP_ROWS), 1)
    chosen = jnp.where(row == wanted[...], 1.0, 0.0).astype(bf16)
    out[...] = dot(chosen, blocks).astype(bf16)


def grant(mebibytes):
    return pltpu.CompilerParams(vmem_limit_bytes=mebibytes * 2**20)


def near(array):
    return pltpu.with_memory_space_constraint(array, pltpu.VMEM)


def shift_y(rows, step):
    return lax.ppermute(rows, "y", [(i, (i + step) % NY) for i in range(NY)])


def shards(grads, right_inv, left_inv, row_signs, col_signs, listed, owners):
    z_id, y_id, c_id, e_id = (lax.axis_index(name) for name in ("z", "y", "c", "e"))
    yc_id = y_id * NC + c_id
    row_id = z_id * NYC + yc_id
    list_len = listed.shape[3]
    capacity = 2

    pieces = pl.pallas_call(
        deal_kernel,
        out_shape=pltpu.VMEM((ROWS, 2 * GROUP_ROWS // NE, BLOCK), bf16),
        in_specs=[IN_VMEM] * 2,
        out_specs=IN_VMEM,
        compiler_params=grant(8),
        name="deal",
    )(right_inv, left_inv)
    pieces = lax.all_to_all(pieces, ROW_AXES, 0, 0, tiled=True)
    pieces = lax.all_to_all(jnp.broadcast_to(pieces[None], (NE,) + pieces.shape), "e", 0, 0, tiled=True)

    swap = [(0, 1), (1, 0)]
    mine = grads.reshape(1, GROUP_ROWS, DM)
    near_rows = jnp.concatenate([shift_y(mine, 1), mine, shift_y(mine, -1)])
    rows_own = jnp.concatenate([shift_y(near_rows, 3), near_rows, shift_y(near_rows[:2], -3)])
    rows_other = lax.ppermute(rows_own, "c", swap)
    factor_shape = pltpu.VMEM((ROWS, GROUP_ROWS, BLOCK), bf16)
    right_cols, left_own = pl.pallas_call(
        arrange_kernel,
        out_shape=(factor_shape, factor_shape),
        in_specs=[IN_VMEM],
        out_specs=(IN_VMEM, IN_VMEM),
        compiler_params=grant(12),
        name="arrange",
    )(near(pieces))
    left_other = lax.ppermute(left_own, "c", swap)
    place = jnp.stack([y_id, c_id])

    row_bits = lax.dynamic_index_in_dim(row_signs[0], e_id, 0, keepdims=False)
    row_flip = (1 - 2 * row_bits).astype(f32)[:, None]
    col_bits = lax.dynamic_index_in_dim(col_signs[0], e_id, 0, keepdims=False)
    col_bits = col_bits.reshape(BLOCK, NYC)
    own_col = jnp.arange(NYC, dtype=jnp.int32) == yc_id
    col_bits = jnp.sum(jnp.where(own_col[None, :], col_bits, 0), axis=1)[None, :]
    col_flip = (1 - 2 * col_bits).astype(f32)
    high, low, twiddles = column_tables()
    tile = pl.pallas_call(
        project_kernel,
        out_shape=pltpu.VMEM((TILE_ROWS, BLOCK), bf16),
        in_specs=[IN_SMEM] + [IN_VMEM] * 4,
        out_specs=IN_VMEM,
        compiler_params=grant(6),
        name="project",
    )(place, near(rows_own), near(rows_other), near(right_cols), col_flip)
    partial_cols = pl.pallas_call(
        whiten_kernel,
        out_shape=pltpu.VMEM((ROWS, 2 * GROUP_ROWS, BLOCK), bf16),
        in_specs=[IN_SMEM] + [IN_VMEM] * 7,
        out_specs=IN_VMEM,
        scratch_shapes=[
            pltpu.VMEM((DM, BLOCK), f32),
            pltpu.VMEM((RADIX, 2 * INNER, BLOCK), f32),
        ],
        compiler_params=grant(16),
        name="whiten",
    )(place, near(tile), near(left_own), near(left_other), row_flip, high, low, twiddles)
    partial_rows = lax.all_to_all(partial_cols, ROW_AXES, 0, 0, tiled=True)

    spectrum_rows = row_id * GROUP_ROWS + jnp.arange(GROUP_ROWS, dtype=jnp.int32)
    columns = jnp.arange(NYC, dtype=jnp.int32)[:, None] + NYC * jnp.arange(BLOCK, dtype=jnp.int32)
    columns = columns.reshape(NYC, 1, BLOCK)
    phase = spectrum_rows[None, :, None] * columns
    angle = phase.astype(f32) * (2.0 * math.pi / (DM * DM))
    cross = jnp.stack([jnp.cos(angle), -jnp.sin(angle)]) * (1.0 / DM)
    local_ids = listed[0, 0, 0] - row_id * (GROUP_ROWS * NYC)
    wanted = (local_ids % NYC) * GROUP_ROWS + local_ids // NYC
    row_high, row_low, turns = row_tables()
    picked = pl.pallas_call(
        spectrum_kernel,
        out_shape=pltpu.VMEM((list_len, 2 * BLOCK), bf16),
        in_specs=[IN_VMEM] * 6,
        out_specs=IN_VMEM,
        scratch_shapes=[pltpu.VMEM((NYC, GROUP_ROWS, 2 * BLOCK), f32)],
        compiler_params=grant(12),
        name="spectrum",
    )(near(partial_rows), near(cross), turns, row_high, row_low, wanted[:, None])

    entries = lax.all_to_all(
        jnp.broadcast_to(picked[None], (NE,) + picked.shape), "e", 0, 0, tiled=True
    ).reshape(NE * list_len, 2 * BLOCK)
    owner_ids = owners[0, 0, :, :, 0].reshape(-1)
    order = jnp.arange(NE * list_len, dtype=jnp.int32)
    same = (owner_ids[:, None] == owner_ids[None, :]) & (order[:, None] < order[None, :])
    position = owner_ids * capacity + jnp.sum(same.astype(jnp.int32), axis=0)
    place = jnp.arange(ROWS * capacity, dtype=jnp.int32)[:, None] == position[None, :]
    outgoing = dot(place.astype(bf16), entries).astype(bf16)
    outgoing = outgoing.reshape(ROWS, capacity, 2 * BLOCK)
    arrived = lax.all_to_all(outgoing, ROW_AXES, 0, 0, tiled=True)
    return arrived.astype(f32)[None, None]


def solution(mesh):
    split = Mesh(mesh.devices.reshape(NZ, NY, NC, NE), ("z", "y", "c", "e"))
    in_specs = (
        P(None, "e", ROW_AXES, None),
        P(ROW_AXES, "e"),
        P(ROW_AXES + ("e",), None),
        P(),
        P(),
        P(None, ROW_AXES, "e", None),
        P(None, ROW_AXES, None, None, None),
    )
    out_specs = P(None, ROW_AXES, None, None, None)
    return jax.shard_map(shards, mesh=split, in_specs=in_specs, out_specs=out_specs, check_vma=False)
```

```python
import math

import jax
import jax.numpy as jnp
import numpy as np
from jax import lax
from jax.experimental import pallas as pl
from jax.experimental.pallas import tpu as pltpu
from jax.sharding import Mesh
from jax.sharding import PartitionSpec as P


DM = 2048
BLOCK = 128
NZ, NY, NC, NE = 8, 8, 2, 4
NYC = NY * NC
ROWS = NZ * NYC
GROUP_ROWS = DM // ROWS
TILE_ROWS = DM // NZ
RADIX = 8
INNER = DM // RADIX
ROOT_HALF = math.sqrt(0.5)

f32 = jnp.float32
bf16 = jnp.bfloat16
ROW_AXES = ("z", "y", "c")
IN_VMEM = pl.BlockSpec(memory_space=pltpu.VMEM)
IN_SMEM = pl.BlockSpec(memory_space=pltpu.SMEM)


def split_table(table):
    high = table.astype(bf16)
    low = (table - high.astype(np.float64)).astype(bf16)
    return high, low


def dft_angles(rows, cols, length):
    return 2.0 * math.pi * ((np.arange(rows)[:, None] * np.arange(cols)[None, :]) % length) / length


def column_tables():
    angles = dft_angles(INNER, INNER, INNER)
    high, low = split_table(np.concatenate([np.cos(angles), -np.sin(angles)], axis=0))
    angles = dft_angles(INNER, RADIX, DM)
    twiddles = np.concatenate([np.cos(angles), -np.sin(angles)], axis=1).astype(np.float32)
    return high, low, twiddles


def row_tables():
    angles = dft_angles(BLOCK, BLOCK, BLOCK)
    real, imag = np.cos(angles), -np.sin(angles)
    full = np.concatenate(
        [np.concatenate([real, imag], axis=1), np.concatenate([-imag, real], axis=1)], axis=0
    )
    high, low = split_table(full)
    angles = dft_angles(NYC, BLOCK, DM)
    twiddles = np.stack([np.cos(angles), -np.sin(angles)]).astype(np.float32)
    return high, low, twiddles.reshape(2, NYC, 1, BLOCK)


def add(a, b):
    return (a[0] + b[0], a[1] + b[1])


def sub(a, b):
    return (a[0] - b[0], a[1] - b[1])


def mul(a, b):
    return (a[0] * b[0] - a[1] * b[1], a[0] * b[1] + a[1] * b[0])


def minus_i(a):
    return (a[1], -a[0])


def fft4(a, b, c, d):
    even, odd = add(a, c), sub(a, c)
    even2, odd2 = add(b, d), minus_i(sub(b, d))
    return [add(even, even2), add(odd, odd2), sub(even, even2), sub(odd, odd2)]


def fft8(terms):
    even = fft4(terms[0], terms[2], terms[4], terms[6])
    odd = fft4(terms[1], terms[3], terms[5], terms[7])
    one = ((odd[1][0] + odd[1][1]) * ROOT_HALF, (odd[1][1] - odd[1][0]) * ROOT_HALF)
    three = ((odd[3][1] - odd[3][0]) * ROOT_HALF, (odd[3][0] + odd[3][1]) * -ROOT_HALF)
    turned = [odd[0], one, minus_i(odd[2]), three]
    return [add(e, o) for e, o in zip(even, turned)] + [sub(e, o) for e, o in zip(even, turned)]


def fft16(terms):
    inner = [fft4(*[terms[4 * a + b] for a in range(4)]) for b in range(4)]
    out = [None] * 16
    for first in range(4):
        column = []
        for b in range(4):
            turn = -2.0 * math.pi * b * first / 16
            value = inner[b][first]
            if b * first:
                cos, sin = math.cos(turn), math.sin(turn)
                value = (value[0] * cos - value[1] * sin, value[0] * sin + value[1] * cos)
            column.append(value)
        for second, value in enumerate(fft4(*column)):
            out[first + 4 * second] = value
    return out


def dot(a, b):
    return jnp.dot(a, b, preferred_element_type=f32)


def deal_kernel(right, left, out):
    quarter = GROUP_ROWS // NE
    width = right.shape[1]
    pack = BLOCK // NE
    column = lax.broadcasted_iota(jnp.int32, (width, width), 0)
    target = lax.broadcasted_iota(jnp.int32, (width, width), 1)
    order = target == pack * (column % NYC) + column // NYC
    sorted_cols = dot(right[...], jnp.where(order, 1.0, 0.0).astype(bf16))
    tail = left[...].astype(f32)
    tail = jnp.concatenate([tail, tail], axis=0)
    shape = (2 * quarter, BLOCK)
    upper = lax.broadcasted_iota(jnp.int32, shape, 0) < quarter
    lane_group = lax.broadcasted_iota(jnp.int32, shape, 1) // pack
    for tile in range(width // BLOCK):
        lanes = slice(tile * BLOCK, (tile + 1) * BLOCK)
        row_groups = []
        for half in range(2):
            value = sorted_cols[2 * quarter * half : 2 * quarter * (half + 1), lanes]
            row_groups += [value, pltpu.roll(value, quarter, axis=0)]
        for group in range(NE):
            yc = tile * NE + group
            piece = None
            for p in range(NE):
                moved = row_groups[p]
                if p != group:
                    moved = pltpu.roll(moved, (pack * (p - group)) % BLOCK, axis=1)
                piece = moved if piece is None else jnp.where(lane_group == p, moved, piece)
            for z in range(NZ):
                zc = z * NC + yc % NC
                both = jnp.where(upper, piece, tail[:, zc * BLOCK : (zc + 1) * BLOCK])
                out[z * NYC + yc] = both.astype(bf16)


def arrange_kernel(pieces, right, left):
    quarter = GROUP_ROWS // NE
    pack = BLOCK // NE
    shape = (ROWS, 2 * quarter, BLOCK)
    first = lax.broadcasted_iota(jnp.int32, shape, 1) < quarter
    lane_group = lax.broadcasted_iota(jnp.int32, shape, 2) // pack
    values = [pieces[e].astype(f32) for e in range(NE)]
    unpacked = []
    for p in range(NE):
        rows = None
        for e in range(NE):
            moved = values[e]
            if e != p:
                moved = pltpu.roll(moved, (pack * (e - p)) % BLOCK, axis=2)
            rows = moved if rows is None else jnp.where(lane_group == e, moved, rows)
        unpacked.append(rows)
    rights, lefts = [], []
    for e in range(0, NE, 2):
        rights.append(jnp.where(first, unpacked[e], pltpu.roll(unpacked[e + 1], quarter, axis=1)))
        lefts.append(jnp.where(first, pltpu.roll(values[e], quarter, axis=1), values[e + 1]))
    right[...] = jnp.concatenate(rights, axis=1).astype(bf16)
    left[...] = jnp.concatenate(lefts, axis=1).astype(bf16)


def project_kernel(place, own, other, right, col_flip, out):
    factor = right[...].reshape(DM, BLOCK)
    for side, rows in enumerate((own, other)):
        part = dot(rows[...].reshape(TILE_ROWS // NC, DM), factor) * col_flip[...]
        part = part.astype(bf16).reshape(NY, GROUP_ROWS, BLOCK)
        for k in range(NY):
            from_y = (place[0] + NY // 2 + k) % NY
            from_c = place[1] if side == 0 else 1 - place[1]
            start = pl.multiple_of(GROUP_ROWS * (NC * from_y + from_c), GROUP_ROWS)
            out[pl.ds(start, GROUP_ROWS), :] = part[k]


def whiten_kernel(place, tile, own, other, row_flip, high, low, twiddles, out, white, stage):
    left = jnp.concatenate([own[...].reshape(DM, BLOCK), other[...].reshape(DM, BLOCK)], axis=1)
    half = TILE_ROWS // NC
    starts = [pl.multiple_of(half * side, half) for side in (place[1], 1 - place[1])]
    halves = [tile[pl.ds(start, half), :] for start in starts]
    white[...] = dot(left, jnp.concatenate(halves, axis=0)) * row_flip[...]
    for p in range(0, RADIX, 2):
        pair = [white[pl.ds(p + k, INNER, stride=RADIX), :] for k in range(2)]
        part = jnp.concatenate(pair, axis=1)
        part_high = part.astype(bf16)
        part_low = (part - part_high.astype(f32)).astype(bf16)
        both = dot(high[...], part_high) + dot(low[...], part_high) + dot(high[...], part_low)
        stage[p] = both[:, 0:BLOCK]
        stage[p + 1] = both[:, BLOCK:]

    def combine(step, carry):
        rows = pl.ds(pl.multiple_of(step * GROUP_ROWS, GROUP_ROWS), GROUP_ROWS)
        rows_imag = pl.ds(pl.multiple_of(INNER + step * GROUP_ROWS, GROUP_ROWS), GROUP_ROWS)
        factors = twiddles[rows, :]
        terms = [(stage[0, rows, :], stage[0, rows_imag, :])]
        for p in range(1, RADIX):
            factor = (factors[:, p : p + 1], factors[:, RADIX + p : RADIX + p + 1])
            terms.append(mul((stage[p, rows, :], stage[p, rows_imag, :]), factor))
        for k, value in enumerate(fft8(terms)):
            out[NYC * k + step, 0:GROUP_ROWS, :] = value[0].astype(bf16)
            out[NYC * k + step, GROUP_ROWS : 2 * GROUP_ROWS, :] = value[1].astype(bf16)
        return carry

    lax.fori_loop(0, INNER // GROUP_ROWS, combine, 0, unroll=4)


def spectrum_kernel(parts, cross, turns, high, low, wanted, out, mixed):
    for yc in range(NYC):
        total = parts[yc].astype(f32)
        for z in range(1, NZ):
            total = total + parts[z * NYC + yc].astype(f32)
        value = mul((total[0:GROUP_ROWS], total[GROUP_ROWS:]), (cross[0, yc], cross[1, yc]))
        mixed[yc, :, 0:BLOCK] = value[0]
        mixed[yc, :, BLOCK : 2 * BLOCK] = value[1]
    rows = mixed[...].reshape(NYC * GROUP_ROWS, 2 * BLOCK)
    rows_high = rows.astype(bf16)
    rows_low = (rows - rows_high.astype(f32)).astype(bf16)
    rows = dot(rows_high, high[...]) + dot(rows_low, high[...]) + dot(rows_high, low[...])
    rows = rows.reshape(NYC, GROUP_ROWS, 2 * BLOCK)
    terms = [
        mul((rows[yc, :, 0:BLOCK], rows[yc, :, BLOCK:]), (turns[0, yc], turns[1, yc]))
        for yc in range(NYC)
    ]
    blocks = [jnp.concatenate(value, axis=1).astype(bf16) for value in fft16(terms)]
    blocks = jnp.concatenate(blocks, axis=0)
    row = lax.broadcasted_iota(jnp.int32, (out.shape[0], NYC * GROUP_ROWS), 1)
    chosen = jnp.where(row == wanted[...], 1.0, 0.0).astype(bf16)
    out[...] = dot(chosen, blocks).astype(bf16)


def grant(mebibytes):
    return pltpu.CompilerParams(vmem_limit_bytes=mebibytes * 2**20)


def near(array):
    return pltpu.with_memory_space_constraint(array, pltpu.VMEM)


def shift_y(rows, step):
    return lax.ppermute(rows, "y", [(i, (i + step) % NY) for i in range(NY)])


def shards(grads, right_inv, left_inv, row_signs, col_signs, listed, owners):
    z_id, y_id, c_id, e_id = (lax.axis_index(name) for name in ("z", "y", "c", "e"))
    yc_id = y_id * NC + c_id
    row_id = z_id * NYC + yc_id
    list_len = listed.shape[3]
    capacity = 2

    pieces = pl.pallas_call(
        deal_kernel,
        out_shape=pltpu.VMEM((ROWS, 2 * GROUP_ROWS // NE, BLOCK), bf16),
        in_specs=[IN_VMEM] * 2,
        out_specs=IN_VMEM,
        compiler_params=grant(8),
        name="deal",
    )(right_inv, left_inv)
    pieces = lax.all_to_all(pieces, ROW_AXES, 0, 0, tiled=True)
    pieces = jnp.broadcast_to(pieces[None], (NE,) + pieces.shape)
    pieces = lax.all_to_all(pieces, "e", 0, 0, tiled=True)

    swap = [(0, 1), (1, 0)]
    mine = grads.reshape(1, GROUP_ROWS, DM)
    near_rows = jnp.concatenate([shift_y(mine, 1), mine, shift_y(mine, -1)])
    far_up, far_down = shift_y(near_rows, 3), shift_y(near_rows[:2], -3)
    rows_own = jnp.concatenate([far_up, near_rows, far_down])
    rows_other = lax.ppermute(rows_own, "c", swap)
    factor_shape = pltpu.VMEM((ROWS, GROUP_ROWS, BLOCK), bf16)
    right_cols, left_own = pl.pallas_call(
        arrange_kernel,
        out_shape=(factor_shape, factor_shape),
        in_specs=[IN_VMEM],
        out_specs=(IN_VMEM, IN_VMEM),
        compiler_params=grant(12),
        name="arrange",
    )(near(pieces))
    left_other = lax.ppermute(left_own, "c", swap)
    place = jnp.stack([y_id, c_id])

    row_bits = lax.dynamic_index_in_dim(row_signs[0], e_id, 0, keepdims=False)
    row_flip = (1 - 2 * row_bits).astype(f32)[:, None]
    col_bits = lax.dynamic_index_in_dim(col_signs[0], e_id, 0, keepdims=False)
    col_bits = col_bits.reshape(BLOCK, NYC)
    own_col = jnp.arange(NYC, dtype=jnp.int32) == yc_id
    col_bits = jnp.sum(jnp.where(own_col[None, :], col_bits, 0), axis=1)[None, :]
    col_flip = (1 - 2 * col_bits).astype(f32)
    high, low, twiddles = column_tables()
    tile = pl.pallas_call(
        project_kernel,
        out_shape=pltpu.VMEM((TILE_ROWS, BLOCK), bf16),
        in_specs=[IN_SMEM] + [IN_VMEM] * 4,
        out_specs=IN_VMEM,
        compiler_params=grant(6),
        name="project",
    )(place, near(rows_own), near(rows_other), near(right_cols), col_flip)
    partial_cols = pl.pallas_call(
        whiten_kernel,
        out_shape=pltpu.VMEM((ROWS, 2 * GROUP_ROWS, BLOCK), bf16),
        in_specs=[IN_SMEM] + [IN_VMEM] * 7,
        out_specs=IN_VMEM,
        scratch_shapes=[
            pltpu.VMEM((DM, BLOCK), f32),
            pltpu.VMEM((RADIX, 2 * INNER, BLOCK), f32),
        ],
        compiler_params=grant(16),
        name="whiten",
    )(place, near(tile), near(left_own), near(left_other), row_flip, high, low, twiddles)
    partial_rows = lax.all_to_all(partial_cols, ROW_AXES, 0, 0, tiled=True)

    spectrum_rows = row_id * GROUP_ROWS + jnp.arange(GROUP_ROWS, dtype=jnp.int32)
    columns = jnp.arange(NYC, dtype=jnp.int32)[:, None] + NYC * jnp.arange(BLOCK, dtype=jnp.int32)
    columns = columns.reshape(NYC, 1, BLOCK)
    phase = spectrum_rows[None, :, None] * columns
    angle = phase.astype(f32) * (2.0 * math.pi / (DM * DM))
    cross = jnp.stack([jnp.cos(angle), -jnp.sin(angle)]) * (1.0 / DM)
    local_ids = listed[0, 0, 0] - row_id * (GROUP_ROWS * NYC)
    wanted = (local_ids % NYC) * GROUP_ROWS + local_ids // NYC
    row_high, row_low, turns = row_tables()
    picked = pl.pallas_call(
        spectrum_kernel,
        out_shape=pltpu.VMEM((list_len, 2 * BLOCK), bf16),
        in_specs=[IN_VMEM] * 6,
        out_specs=IN_VMEM,
        scratch_shapes=[pltpu.VMEM((NYC, GROUP_ROWS, 2 * BLOCK), f32)],
        compiler_params=grant(12),
        name="spectrum",
    )(near(partial_rows), near(cross), turns, row_high, row_low, wanted[:, None])

    entries = lax.all_to_all(
        jnp.broadcast_to(picked[None], (NE,) + picked.shape), "e", 0, 0, tiled=True
    ).reshape(NE * list_len, 2 * BLOCK)
    owner_ids = owners[0, 0, :, :, 0].reshape(-1)
    order = jnp.arange(NE * list_len, dtype=jnp.int32)
    same = (owner_ids[:, None] == owner_ids[None, :]) & (order[:, None] < order[None, :])
    position = owner_ids * capacity + jnp.sum(same.astype(jnp.int32), axis=0)
    place = jnp.arange(ROWS * capacity, dtype=jnp.int32)[:, None] == position[None, :]
    outgoing = dot(place.astype(bf16), entries).astype(bf16)
    outgoing = outgoing.reshape(ROWS, capacity, 2 * BLOCK)
    arrived = lax.all_to_all(outgoing, ROW_AXES, 0, 0, tiled=True)
    return arrived.astype(f32)[None, None]


def solution(mesh):
    split = Mesh(mesh.devices.reshape(NZ, NY, NC, NE), ("z", "y", "c", "e"))
    in_specs = (
        P(None, "e", ROW_AXES, None),
        P(ROW_AXES, "e"),
        P(ROW_AXES + ("e",), None),
        P(),
        P(),
        P(None, ROW_AXES, "e", None),
        P(None, ROW_AXES, None, None, None),
    )
    out_specs = P(None, ROW_AXES, None, None, None)
    return jax.shard_map(shards, mesh=split, in_specs=in_specs, out_specs=out_specs, check_vma=False)
```

```python
import math

import jax
import jax.numpy as jnp
import numpy as np
from jax import lax
from jax.experimental import pallas as pl
from jax.experimental.pallas import tpu as pltpu
from jax.sharding import Mesh
from jax.sharding import PartitionSpec as P


DM = 2048
BLOCK = 128
NZ, NY, NC, NE = 8, 8, 2, 4
NYC = NY * NC
ROWS = NZ * NYC
GROUP_ROWS = DM // ROWS
TILE_ROWS = DM // NZ
RADIX = 8
INNER = DM // RADIX
ROOT_HALF = math.sqrt(0.5)

f32 = jnp.float32
bf16 = jnp.bfloat16
ROW_AXES = ("z", "y", "c")
IN_VMEM = pl.BlockSpec(memory_space=pltpu.VMEM)
IN_SMEM = pl.BlockSpec(memory_space=pltpu.SMEM)


def split_table(table):
    high = table.astype(bf16)
    low = (table - high.astype(np.float64)).astype(bf16)
    return [high, low]


def split_values(values):
    high = values.astype(bf16)
    return [high, (values - high.astype(f32)).astype(bf16)]


def dft_angles(rows, cols, length):
    return 2.0 * math.pi * ((np.arange(rows)[:, None] * np.arange(cols)[None, :]) % length) / length


def column_tables():
    angles = dft_angles(INNER, INNER, INNER)
    high, low = split_table(np.concatenate([np.cos(angles), -np.sin(angles)], axis=0))
    angles = dft_angles(INNER, RADIX, DM)
    twiddles = np.concatenate([np.cos(angles), -np.sin(angles)], axis=1).astype(np.float32)
    return np.concatenate([high, low, high], axis=1), twiddles


def row_tables():
    angles = dft_angles(BLOCK, BLOCK, BLOCK)
    real, imag = np.cos(angles), -np.sin(angles)
    full = np.concatenate(
        [np.concatenate([real, imag], axis=1), np.concatenate([-imag, real], axis=1)], axis=0
    )
    high, low = split_table(full)
    angles = dft_angles(NYC, BLOCK, DM)
    twiddles = np.stack([np.cos(angles), -np.sin(angles)]).astype(np.float32)
    return np.concatenate([high, low, high], axis=0), twiddles.reshape(2, NYC, 1, BLOCK)


def add(a, b):
    return (a[0] + b[0], a[1] + b[1])


def sub(a, b):
    return (a[0] - b[0], a[1] - b[1])


def mul(a, b):
    return (a[0] * b[0] - a[1] * b[1], a[0] * b[1] + a[1] * b[0])


def minus_i(a):
    return (a[1], -a[0])


def fft4(a, b, c, d):
    even, odd = add(a, c), sub(a, c)
    even2, odd2 = add(b, d), minus_i(sub(b, d))
    return [add(even, even2), add(odd, odd2), sub(even, even2), sub(odd, odd2)]


def fft8(terms):
    even = fft4(terms[0], terms[2], terms[4], terms[6])
    odd = fft4(terms[1], terms[3], terms[5], terms[7])
    one = ((odd[1][0] + odd[1][1]) * ROOT_HALF, (odd[1][1] - odd[1][0]) * ROOT_HALF)
    three = ((odd[3][1] - odd[3][0]) * ROOT_HALF, (odd[3][0] + odd[3][1]) * -ROOT_HALF)
    turned = [odd[0], one, minus_i(odd[2]), three]
    return [add(e, o) for e, o in zip(even, turned)] + [sub(e, o) for e, o in zip(even, turned)]


def fft16(terms):
    inner = [fft4(*[terms[4 * a + b] for a in range(4)]) for b in range(4)]
    out = [None] * 16
    for first in range(4):
        column = []
        for b in range(4):
            turn = -2.0 * math.pi * b * first / 16
            value = inner[b][first]
            if b * first:
                cos, sin = math.cos(turn), math.sin(turn)
                value = (value[0] * cos - value[1] * sin, value[0] * sin + value[1] * cos)
            column.append(value)
        for second, value in enumerate(fft4(*column)):
            out[first + 4 * second] = value
    return out


def dot(a, b):
    return jnp.dot(a, b, preferred_element_type=f32)


def deal_kernel(right_far, left_far, out, right, left, arrived):
    copies = [
        pltpu.make_async_copy(right_far, right, arrived.at[0]),
        pltpu.make_async_copy(left_far, left, arrived.at[1]),
    ]
    for copy in copies:
        copy.start()
    for copy in copies:
        copy.wait()
    quarter = GROUP_ROWS // NE
    width = right.shape[1]
    pack = BLOCK // NE
    column = lax.broadcasted_iota(jnp.int32, (width, width), 0)
    target = lax.broadcasted_iota(jnp.int32, (width, width), 1)
    order = target == pack * (column % NYC) + column // NYC
    sorted_cols = dot(right[...], jnp.where(order, 1.0, 0.0).astype(bf16))
    tail = left[...].astype(f32)
    tail = jnp.concatenate([tail, tail], axis=0)
    shape = (2 * quarter, BLOCK)
    upper = lax.broadcasted_iota(jnp.int32, shape, 0) < quarter
    lane_group = lax.broadcasted_iota(jnp.int32, shape, 1) // pack
    for tile in range(width // BLOCK):
        lanes = slice(tile * BLOCK, (tile + 1) * BLOCK)
        row_groups = []
        for half in range(2):
            value = sorted_cols[2 * quarter * half : 2 * quarter * (half + 1), lanes]
            row_groups += [value, pltpu.roll(value, quarter, axis=0)]
        for group in range(NE):
            yc = tile * NE + group
            piece = None
            for p in range(NE):
                moved = row_groups[p]
                if p != group:
                    moved = pltpu.roll(moved, (pack * (p - group)) % BLOCK, axis=1)
                piece = moved if piece is None else jnp.where(lane_group == p, moved, piece)
            for z in range(NZ):
                zc = z * NC + yc % NC
                both = jnp.where(upper, piece, tail[:, zc * BLOCK : (zc + 1) * BLOCK])
                out[z * NYC + yc] = both.astype(bf16)


def arrange_kernel(pieces, right, left):
    quarter = GROUP_ROWS // NE
    pack = BLOCK // NE
    shape = (ROWS, 2 * quarter, BLOCK)
    first = lax.broadcasted_iota(jnp.int32, shape, 1) < quarter
    lane_group = lax.broadcasted_iota(jnp.int32, shape, 2) // pack
    values = [pieces[e].astype(f32) for e in range(NE)]
    unpacked = []
    for p in range(NE):
        rows = None
        for e in range(NE):
            moved = values[e]
            if e != p:
                moved = pltpu.roll(moved, (pack * (e - p)) % BLOCK, axis=2)
            rows = moved if rows is None else jnp.where(lane_group == e, moved, rows)
        unpacked.append(rows)
    rights, lefts = [], []
    for e in range(0, NE, 2):
        rights.append(jnp.where(first, unpacked[e], pltpu.roll(unpacked[e + 1], quarter, axis=1)))
        lefts.append(jnp.where(first, pltpu.roll(values[e], quarter, axis=1), values[e + 1]))
    right[...] = jnp.concatenate(rights, axis=1).astype(bf16)
    left[...] = jnp.concatenate(lefts, axis=1).astype(bf16)


def project_kernel(place, own, other, right, col_flip, out):
    factor = right[...].reshape(DM, BLOCK)
    for side, rows in enumerate((own, other)):
        part = dot(rows[...].reshape(TILE_ROWS // NC, DM), factor) * col_flip[...]
        part = part.astype(bf16).reshape(NY, GROUP_ROWS, BLOCK)
        for k in range(NY):
            from_y = (place[0] + NY // 2 + k) % NY
            from_c = place[1] if side == 0 else 1 - place[1]
            start = pl.multiple_of(GROUP_ROWS * (NC * from_y + from_c), GROUP_ROWS)
            out[pl.ds(start, GROUP_ROWS), :] = part[k]


def whiten_kernel(place, tile, own, other, row_flip, table, twiddles, out, white, stage):
    left = jnp.concatenate([own[...].reshape(DM, BLOCK), other[...].reshape(DM, BLOCK)], axis=1)
    half = TILE_ROWS // NC
    starts = [pl.multiple_of(half * side, half) for side in (place[1], 1 - place[1])]
    halves = [tile[pl.ds(start, half), :] for start in starts]
    white[...] = dot(left, jnp.concatenate(halves, axis=0)) * row_flip[...]
    for p in range(0, RADIX, 2):
        pair = [white[pl.ds(p + k, INNER, stride=RADIX), :] for k in range(2)]
        part = jnp.concatenate(pair, axis=1)
        part_high, part_low = split_values(part)
        both = dot(table[...], jnp.concatenate([part_high, part_high, part_low], axis=0))
        stage[p] = both[:, 0:BLOCK]
        stage[p + 1] = both[:, BLOCK:]

    def combine(step, carry):
        rows = pl.ds(pl.multiple_of(step * GROUP_ROWS, GROUP_ROWS), GROUP_ROWS)
        rows_imag = pl.ds(pl.multiple_of(INNER + step * GROUP_ROWS, GROUP_ROWS), GROUP_ROWS)
        factors = twiddles[rows, :]
        terms = [(stage[0, rows, :], stage[0, rows_imag, :])]
        for p in range(1, RADIX):
            factor = (factors[:, p : p + 1], factors[:, RADIX + p : RADIX + p + 1])
            terms.append(mul((stage[p, rows, :], stage[p, rows_imag, :]), factor))
        for k, value in enumerate(fft8(terms)):
            out[NYC * k + step, 0:GROUP_ROWS, :] = value[0].astype(bf16)
            out[NYC * k + step, GROUP_ROWS : 2 * GROUP_ROWS, :] = value[1].astype(bf16)
        return carry

    lax.fori_loop(0, INNER // GROUP_ROWS, combine, 0, unroll=4)


def spectrum_kernel(parts, cross, turns, table, wanted, out, mixed):
    for yc in range(NYC):
        total = parts[yc].astype(f32)
        for z in range(1, NZ):
            total = total + parts[z * NYC + yc].astype(f32)
        value = mul((total[0:GROUP_ROWS], total[GROUP_ROWS:]), (cross[0, yc], cross[1, yc]))
        mixed[yc, :, 0:BLOCK] = value[0]
        mixed[yc, :, BLOCK : 2 * BLOCK] = value[1]
    rows = mixed[...].reshape(NYC * GROUP_ROWS, 2 * BLOCK)
    rows_high, rows_low = split_values(rows)
    rows = dot(jnp.concatenate([rows_high, rows_high, rows_low], axis=1), table[...])
    rows = rows.reshape(NYC, GROUP_ROWS, 2 * BLOCK)
    terms = [
        mul((rows[yc, :, 0:BLOCK], rows[yc, :, BLOCK:]), (turns[0, yc], turns[1, yc]))
        for yc in range(NYC)
    ]
    blocks = [jnp.concatenate(value, axis=1).astype(bf16) for value in fft16(terms)]
    blocks = jnp.concatenate(blocks, axis=0)
    row = lax.broadcasted_iota(jnp.int32, (out.shape[0], NYC * GROUP_ROWS), 1)
    chosen = jnp.where(row == wanted[...], 1.0, 0.0).astype(bf16)
    out[...] = dot(chosen, blocks).astype(bf16)


def grant(mebibytes):
    return pltpu.CompilerParams(vmem_limit_bytes=mebibytes * 2**20)


def near(array):
    return pltpu.with_memory_space_constraint(array, pltpu.VMEM)


def shift_y(rows, step):
    return lax.ppermute(rows, "y", [(i, (i + step) % NY) for i in range(NY)])


def shards(grads, right_inv, left_inv, row_signs, col_signs, listed, owners):
    z_id, y_id, c_id, e_id = (lax.axis_index(name) for name in ("z", "y", "c", "e"))
    yc_id = y_id * NC + c_id
    row_id = z_id * NYC + yc_id
    list_len = listed.shape[3]
    capacity = 2

    pieces = pl.pallas_call(
        deal_kernel,
        out_shape=jax.ShapeDtypeStruct((ROWS, 2 * GROUP_ROWS // NE, BLOCK), bf16),
        in_specs=[pl.BlockSpec(memory_space=pl.ANY)] * 2,
        scratch_shapes=[
            pltpu.VMEM(right_inv.shape, bf16),
            pltpu.VMEM(left_inv.shape, bf16),
            pltpu.SemaphoreType.DMA((2,)),
        ],
        compiler_params=grant(8),
        name="deal",
    )(right_inv, left_inv)
    pieces = lax.all_to_all(pieces, ROW_AXES, 0, 0, tiled=True)
    pieces = jnp.broadcast_to(pieces[None], (NE,) + pieces.shape)
    pieces = lax.all_to_all(pieces, "e", 0, 0, tiled=True)

    swap = [(0, 1), (1, 0)]
    mine = grads.reshape(1, GROUP_ROWS, DM)
    near_rows = jnp.concatenate([shift_y(mine, 1), mine, shift_y(mine, -1)])
    far_up, far_down = shift_y(near_rows, 3), shift_y(near_rows[:2], -3)
    rows_own = jnp.concatenate([far_up, near_rows, far_down])
    rows_other = lax.ppermute(rows_own, "c", swap)
    factor_shape = pltpu.VMEM((ROWS, GROUP_ROWS, BLOCK), bf16)
    right_cols, left_own = pl.pallas_call(
        arrange_kernel,
        out_shape=(factor_shape, factor_shape),
        in_specs=[IN_VMEM],
        out_specs=(IN_VMEM, IN_VMEM),
        compiler_params=grant(12),
        name="arrange",
    )(near(pieces))
    left_other = lax.ppermute(left_own, "c", swap)
    place = jnp.stack([y_id, c_id])

    row_bits = lax.dynamic_index_in_dim(row_signs[0], e_id, 0, keepdims=False)
    row_flip = (1 - 2 * row_bits).astype(f32)[:, None]
    col_bits = lax.dynamic_index_in_dim(col_signs[0], e_id, 0, keepdims=False)
    col_bits = col_bits.reshape(BLOCK, NYC)
    own_col = jnp.arange(NYC, dtype=jnp.int32) == yc_id
    col_bits = jnp.sum(jnp.where(own_col[None, :], col_bits, 0), axis=1)[None, :]
    col_flip = (1 - 2 * col_bits).astype(f32)
    spectrum_rows = row_id * GROUP_ROWS + jnp.arange(GROUP_ROWS, dtype=jnp.int32)
    columns = jnp.arange(NYC, dtype=jnp.int32)[:, None] + NYC * jnp.arange(BLOCK, dtype=jnp.int32)
    columns = columns.reshape(NYC, 1, BLOCK)
    phase = spectrum_rows[None, :, None] * columns
    angle = phase.astype(f32) * (2.0 * math.pi / (DM * DM))
    cross = jnp.stack([jnp.cos(angle), -jnp.sin(angle)]) * (1.0 / DM)
    local_ids = listed[0, 0, 0] - row_id * (GROUP_ROWS * NYC)
    wanted = (local_ids % NYC) * GROUP_ROWS + local_ids // NYC
    wanted = wanted[:, None]
    owner_ids = owners[0, 0, :, :, 0].reshape(-1)
    order = jnp.arange(NE * list_len, dtype=jnp.int32)
    same = (owner_ids[:, None] == owner_ids[None, :]) & (order[:, None] < order[None, :])
    position = owner_ids * capacity + jnp.sum(same.astype(jnp.int32), axis=0)
    column_table, twiddles = column_tables()
    tile = pl.pallas_call(
        project_kernel,
        out_shape=pltpu.VMEM((TILE_ROWS, BLOCK), bf16),
        in_specs=[IN_SMEM] + [IN_VMEM] * 4,
        out_specs=IN_VMEM,
        compiler_params=grant(6),
        name="project",
    )(place, near(rows_own), near(rows_other), near(right_cols), col_flip)
    partial_cols = pl.pallas_call(
        whiten_kernel,
        out_shape=pltpu.VMEM((ROWS, 2 * GROUP_ROWS, BLOCK), bf16),
        in_specs=[IN_SMEM] + [IN_VMEM] * 6,
        out_specs=IN_VMEM,
        scratch_shapes=[
            pltpu.VMEM((DM, BLOCK), f32),
            pltpu.VMEM((RADIX, 2 * INNER, BLOCK), f32),
        ],
        compiler_params=grant(16),
        name="whiten",
    )(place, near(tile), near(left_own), near(left_other), row_flip, column_table, twiddles)
    partial_rows = lax.all_to_all(partial_cols, ROW_AXES, 0, 0, tiled=True)

    row_table, turns = row_tables()
    picked = pl.pallas_call(
        spectrum_kernel,
        out_shape=pltpu.VMEM((list_len, 2 * BLOCK), bf16),
        in_specs=[IN_VMEM] * 5,
        out_specs=IN_VMEM,
        scratch_shapes=[pltpu.VMEM((NYC, GROUP_ROWS, 2 * BLOCK), f32)],
        compiler_params=grant(12),
        name="spectrum",
    )(near(partial_rows), near(cross), turns, row_table, wanted)

    entries = lax.all_to_all(
        jnp.broadcast_to(picked[None], (NE,) + picked.shape), "e", 0, 0, tiled=True
    ).reshape(NE * list_len, 2 * BLOCK)
    place = jnp.arange(ROWS * capacity, dtype=jnp.int32)[:, None] == position[None, :]
    outgoing = dot(place.astype(bf16), entries).astype(bf16)
    outgoing = outgoing.reshape(ROWS, capacity, 2 * BLOCK)
    arrived = lax.all_to_all(outgoing, ROW_AXES, 0, 0, tiled=True)
    return arrived.astype(f32)[None, None]


def solution(mesh):
    split = Mesh(mesh.devices.reshape(NZ, NY, NC, NE), ("z", "y", "c", "e"))
    in_specs = (
        P(None, "e", ROW_AXES, None),
        P(ROW_AXES, "e"),
        P(ROW_AXES + ("e",), None),
        P(),
        P(),
        P(None, ROW_AXES, "e", None),
        P(None, ROW_AXES, None, None, None),
    )
    out_specs = P(None, ROW_AXES, None, None, None)
    return jax.shard_map(shards, mesh=split, in_specs=in_specs, out_specs=out_specs, check_vma=False)
```

```python
import math

import jax
import jax.numpy as jnp
import numpy as np
from jax import lax
from jax.experimental import pallas as pl
from jax.experimental.pallas import tpu as pltpu
from jax.sharding import Mesh
from jax.sharding import PartitionSpec as P


DM = 2048
BLOCK = 128
NZ, NY, NC, NE = 8, 8, 2, 4
NYC = NY * NC
ROWS = NZ * NYC
GROUP_ROWS = DM // ROWS
TILE_ROWS = DM // NZ
RADIX = 8
INNER = DM // RADIX
ROOT_HALF = math.sqrt(0.5)

f32 = jnp.float32
bf16 = jnp.bfloat16
ROW_AXES = ("z", "y", "c")
IN_VMEM = pl.BlockSpec(memory_space=pltpu.VMEM)
IN_SMEM = pl.BlockSpec(memory_space=pltpu.SMEM)


def split_table(table):
    high = table.astype(bf16)
    low = (table - high.astype(np.float64)).astype(bf16)
    return [high, low]


def split_values(values):
    high = values.astype(bf16)
    return [high, (values - high.astype(f32)).astype(bf16)]


def dft_angles(rows, cols, length):
    return 2.0 * math.pi * ((np.arange(rows)[:, None] * np.arange(cols)[None, :]) % length) / length


def column_tables():
    angles = dft_angles(INNER, INNER, INNER)
    high, low = split_table(np.concatenate([np.cos(angles), -np.sin(angles)], axis=0))
    angles = dft_angles(INNER, RADIX, DM)
    twiddles = np.concatenate([np.cos(angles), -np.sin(angles)], axis=1).astype(np.float32)
    return np.concatenate([high, low, high], axis=1), twiddles


def row_tables():
    angles = dft_angles(BLOCK, BLOCK, BLOCK)
    real, imag = np.cos(angles), -np.sin(angles)
    full = np.concatenate(
        [np.concatenate([real, imag], axis=1), np.concatenate([-imag, real], axis=1)], axis=0
    )
    high, low = split_table(full)
    angles = dft_angles(NYC, BLOCK, DM)
    twiddles = np.stack([np.cos(angles), -np.sin(angles)]).astype(np.float32)
    return np.concatenate([high, low, high], axis=0), twiddles.reshape(2, NYC, 1, BLOCK)


def add(a, b):
    return (a[0] + b[0], a[1] + b[1])


def sub(a, b):
    return (a[0] - b[0], a[1] - b[1])


def mul(a, b):
    return (a[0] * b[0] - a[1] * b[1], a[0] * b[1] + a[1] * b[0])


def minus_i(a):
    return (a[1], -a[0])


def fft4(a, b, c, d):
    even, odd = add(a, c), sub(a, c)
    even2, odd2 = add(b, d), minus_i(sub(b, d))
    return [add(even, even2), add(odd, odd2), sub(even, even2), sub(odd, odd2)]


def fft8(terms):
    even = fft4(terms[0], terms[2], terms[4], terms[6])
    odd = fft4(terms[1], terms[3], terms[5], terms[7])
    one = ((odd[1][0] + odd[1][1]) * ROOT_HALF, (odd[1][1] - odd[1][0]) * ROOT_HALF)
    three = ((odd[3][1] - odd[3][0]) * ROOT_HALF, (odd[3][0] + odd[3][1]) * -ROOT_HALF)
    turned = [odd[0], one, minus_i(odd[2]), three]
    return [add(e, o) for e, o in zip(even, turned)] + [sub(e, o) for e, o in zip(even, turned)]


def fft16(terms):
    inner = [fft4(*[terms[4 * a + b] for a in range(4)]) for b in range(4)]
    out = [None] * 16
    for first in range(4):
        column = []
        for b in range(4):
            turn = -2.0 * math.pi * b * first / 16
            value = inner[b][first]
            if b * first:
                cos, sin = math.cos(turn), math.sin(turn)
                value = (value[0] * cos - value[1] * sin, value[0] * sin + value[1] * cos)
            column.append(value)
        for second, value in enumerate(fft4(*column)):
            out[first + 4 * second] = value
    return out


def dot(a, b):
    return jnp.dot(a, b, preferred_element_type=f32)


def deal_kernel(right_far, left_far, out, right, left, arrived):
    copies = [
        pltpu.make_async_copy(right_far, right, arrived.at[0]),
        pltpu.make_async_copy(left_far, left, arrived.at[1]),
    ]
    for copy in copies:
        copy.start()
    for copy in copies:
        copy.wait()
    quarter = GROUP_ROWS // NE
    width = right.shape[1]
    pack = BLOCK // NE
    column = lax.broadcasted_iota(jnp.int32, (width, width), 0)
    target = lax.broadcasted_iota(jnp.int32, (width, width), 1)
    order = target == pack * (column % NYC) + column // NYC
    sorted_cols = dot(right[...], jnp.where(order, 1.0, 0.0).astype(bf16))
    tail = left[...].astype(f32)
    tail = jnp.concatenate([tail, tail], axis=0)
    shape = (2 * quarter, BLOCK)
    upper = lax.broadcasted_iota(jnp.int32, shape, 0) < quarter
    lane_group = lax.broadcasted_iota(jnp.int32, shape, 1) // pack
    for tile in range(width // BLOCK):
        lanes = slice(tile * BLOCK, (tile + 1) * BLOCK)
        row_groups = []
        for half in range(2):
            value = sorted_cols[2 * quarter * half : 2 * quarter * (half + 1), lanes]
            row_groups += [value, pltpu.roll(value, quarter, axis=0)]
        for group in range(NE):
            yc = tile * NE + group
            piece = None
            for p in range(NE):
                moved = row_groups[p]
                if p != group:
                    moved = pltpu.roll(moved, (pack * (p - group)) % BLOCK, axis=1)
                piece = moved if piece is None else jnp.where(lane_group == p, moved, piece)
            for z in range(NZ):
                zc = z * NC + yc % NC
                both = jnp.where(upper, piece, tail[:, zc * BLOCK : (zc + 1) * BLOCK])
                out[z * NYC + yc] = both.astype(bf16)


def arrange_kernel(pieces, right, left):
    quarter = GROUP_ROWS // NE
    pack = BLOCK // NE
    shape = (ROWS, 2 * quarter, BLOCK)
    first = lax.broadcasted_iota(jnp.int32, shape, 1) < quarter
    lane_group = lax.broadcasted_iota(jnp.int32, shape, 2) // pack
    values = [pieces[e].astype(f32) for e in range(NE)]
    unpacked = []
    for p in range(NE):
        rows = None
        for e in range(NE):
            moved = values[e]
            if e != p:
                moved = pltpu.roll(moved, (pack * (e - p)) % BLOCK, axis=2)
            rows = moved if rows is None else jnp.where(lane_group == e, moved, rows)
        unpacked.append(rows)
    rights, lefts = [], []
    for e in range(0, NE, 2):
        rights.append(jnp.where(first, unpacked[e], pltpu.roll(unpacked[e + 1], quarter, axis=1)))
        lefts.append(jnp.where(first, pltpu.roll(values[e], quarter, axis=1), values[e + 1]))
    right[...] = jnp.concatenate(rights, axis=1).astype(bf16)
    left[...] = jnp.concatenate(lefts, axis=1).astype(bf16)


def join_kernel(far_up, middle, far_down, out):
    out[0:3] = far_up[...]
    out[3:6] = middle[...]
    out[6:8] = far_down[...]


def project_kernel(place, own, other, right, col_flip, out):
    factor = right[...].reshape(DM, BLOCK)
    for side, rows in enumerate((own, other)):
        part = dot(rows[...].reshape(TILE_ROWS // NC, DM), factor) * col_flip[...]
        part = part.astype(bf16).reshape(NY, GROUP_ROWS, BLOCK)
        for k in range(NY):
            from_y = (place[0] + NY // 2 + k) % NY
            from_c = place[1] if side == 0 else 1 - place[1]
            start = pl.multiple_of(GROUP_ROWS * (NC * from_y + from_c), GROUP_ROWS)
            out[pl.ds(start, GROUP_ROWS), :] = part[k]


def whiten_kernel(place, tile, own, other, row_flip, table, twiddles, out, white, stage):
    left = jnp.concatenate([own[...].reshape(DM, BLOCK), other[...].reshape(DM, BLOCK)], axis=1)
    half = TILE_ROWS // NC
    starts = [pl.multiple_of(half * side, half) for side in (place[1], 1 - place[1])]
    halves = [tile[pl.ds(start, half), :] for start in starts]
    white[...] = dot(left, jnp.concatenate(halves, axis=0)) * row_flip[...]
    for p in range(0, RADIX, 2):
        pair = [white[pl.ds(p + k, INNER, stride=RADIX), :] for k in range(2)]
        part = jnp.concatenate(pair, axis=1)
        part_high, part_low = split_values(part)
        both = dot(table[...], jnp.concatenate([part_high, part_high, part_low], axis=0))
        stage[p] = both[:, 0:BLOCK]
        stage[p + 1] = both[:, BLOCK:]

    def combine(step, carry):
        rows = pl.ds(pl.multiple_of(step * GROUP_ROWS, GROUP_ROWS), GROUP_ROWS)
        rows_imag = pl.ds(pl.multiple_of(INNER + step * GROUP_ROWS, GROUP_ROWS), GROUP_ROWS)
        factors = twiddles[rows, :]
        terms = [(stage[0, rows, :], stage[0, rows_imag, :])]
        for p in range(1, RADIX):
            factor = (factors[:, p : p + 1], factors[:, RADIX + p : RADIX + p + 1])
            terms.append(mul((stage[p, rows, :], stage[p, rows_imag, :]), factor))
        for k, value in enumerate(fft8(terms)):
            out[NYC * k + step, 0:GROUP_ROWS, :] = value[0].astype(bf16)
            out[NYC * k + step, GROUP_ROWS : 2 * GROUP_ROWS, :] = value[1].astype(bf16)
        return carry

    lax.fori_loop(0, INNER // GROUP_ROWS, combine, 0, unroll=4)


def spectrum_kernel(parts, cross, turns, table, wanted, out, mixed):
    for yc in range(NYC):
        total = parts[yc].astype(f32)
        for z in range(1, NZ):
            total = total + parts[z * NYC + yc].astype(f32)
        value = mul((total[0:GROUP_ROWS], total[GROUP_ROWS:]), (cross[0, yc], cross[1, yc]))
        mixed[yc, :, 0:BLOCK] = value[0]
        mixed[yc, :, BLOCK : 2 * BLOCK] = value[1]
    rows = mixed[...].reshape(NYC * GROUP_ROWS, 2 * BLOCK)
    rows_high, rows_low = split_values(rows)
    rows = dot(jnp.concatenate([rows_high, rows_high, rows_low], axis=1), table[...])
    rows = rows.reshape(NYC, GROUP_ROWS, 2 * BLOCK)
    terms = [
        mul((rows[yc, :, 0:BLOCK], rows[yc, :, BLOCK:]), (turns[0, yc], turns[1, yc]))
        for yc in range(NYC)
    ]
    blocks = [jnp.concatenate(value, axis=1).astype(bf16) for value in fft16(terms)]
    blocks = jnp.concatenate(blocks, axis=0)
    row = lax.broadcasted_iota(jnp.int32, (out.shape[0], NYC * GROUP_ROWS), 1)
    chosen = jnp.where(row == wanted[...], 1.0, 0.0).astype(bf16)
    out[...] = dot(chosen, blocks).astype(bf16)


def grant(mebibytes):
    return pltpu.CompilerParams(vmem_limit_bytes=mebibytes * 2**20)


def near(array):
    return pltpu.with_memory_space_constraint(array, pltpu.VMEM)


def far(array):
    return pltpu.with_memory_space_constraint(array, pltpu.HBM)


def shift_y(rows, step):
    return lax.ppermute(rows, "y", [(i, (i + step) % NY) for i in range(NY)])


def shards(grads, right_inv, left_inv, row_signs, col_signs, listed, owners):
    z_id, y_id, c_id, e_id = (lax.axis_index(name) for name in ("z", "y", "c", "e"))
    yc_id = y_id * NC + c_id
    row_id = z_id * NYC + yc_id
    list_len = listed.shape[3]
    capacity = 2

    pieces = pl.pallas_call(
        deal_kernel,
        out_shape=jax.ShapeDtypeStruct((ROWS, 2 * GROUP_ROWS // NE, BLOCK), bf16),
        in_specs=[pl.BlockSpec(memory_space=pl.ANY)] * 2,
        scratch_shapes=[
            pltpu.VMEM(right_inv.shape, bf16),
            pltpu.VMEM(left_inv.shape, bf16),
            pltpu.SemaphoreType.DMA((2,)),
        ],
        compiler_params=grant(8),
        name="deal",
    )(far(right_inv), far(left_inv))
    pieces = lax.all_to_all(pieces, ROW_AXES, 0, 0, tiled=True)
    pieces = jnp.broadcast_to(pieces[None], (NE,) + pieces.shape)
    pieces = lax.all_to_all(pieces, "e", 0, 0, tiled=True)

    swap = [(0, 1), (1, 0)]
    mine = grads.reshape(1, GROUP_ROWS, DM)
    near_rows = jnp.concatenate([shift_y(mine, 1), mine, shift_y(mine, -1)])
    far_up, far_down = shift_y(near_rows, 3), shift_y(near_rows[:2], -3)
    rows_own = pl.pallas_call(
        join_kernel,
        out_shape=pltpu.VMEM((NY, GROUP_ROWS, DM), bf16),
        in_specs=[IN_VMEM] * 3,
        out_specs=IN_VMEM,
        compiler_params=grant(4),
        name="join",
    )(near(far_up), near(near_rows), near(far_down))
    rows_other = lax.ppermute(rows_own, "c", swap)
    factor_shape = pltpu.VMEM((ROWS, GROUP_ROWS, BLOCK), bf16)
    right_cols, left_own = pl.pallas_call(
        arrange_kernel,
        out_shape=(factor_shape, factor_shape),
        in_specs=[IN_VMEM],
        out_specs=(IN_VMEM, IN_VMEM),
        compiler_params=grant(12),
        name="arrange",
    )(near(pieces))
    left_other = lax.ppermute(left_own, "c", swap)
    place = jnp.stack([y_id, c_id])

    row_bits = lax.dynamic_index_in_dim(row_signs[0], e_id, 0, keepdims=False)
    row_flip = (1 - 2 * row_bits).astype(f32)[:, None]
    col_bits = lax.dynamic_index_in_dim(col_signs[0], e_id, 0, keepdims=False)
    col_bits = col_bits.reshape(BLOCK, NYC)
    own_col = jnp.arange(NYC, dtype=jnp.int32) == yc_id
    col_bits = jnp.sum(jnp.where(own_col[None, :], col_bits, 0), axis=1)[None, :]
    col_flip = (1 - 2 * col_bits).astype(f32)
    spectrum_rows = row_id * GROUP_ROWS + jnp.arange(GROUP_ROWS, dtype=jnp.int32)
    columns = jnp.arange(NYC, dtype=jnp.int32)[:, None] + NYC * jnp.arange(BLOCK, dtype=jnp.int32)
    columns = columns.reshape(NYC, 1, BLOCK)
    phase = spectrum_rows[None, :, None] * columns
    angle = phase.astype(f32) * (2.0 * math.pi / (DM * DM))
    cross = jnp.stack([jnp.cos(angle), -jnp.sin(angle)]) * (1.0 / DM)
    local_ids = listed[0, 0, 0] - row_id * (GROUP_ROWS * NYC)
    wanted = (local_ids % NYC) * GROUP_ROWS + local_ids // NYC
    wanted = wanted[:, None]
    owner_ids = owners[0, 0, :, :, 0].reshape(-1)
    order = jnp.arange(NE * list_len, dtype=jnp.int32)
    same = (owner_ids[:, None] == owner_ids[None, :]) & (order[:, None] < order[None, :])
    position = owner_ids * capacity + jnp.sum(same.astype(jnp.int32), axis=0)
    column_table, twiddles = column_tables()
    tile = pl.pallas_call(
        project_kernel,
        out_shape=pltpu.VMEM((TILE_ROWS, BLOCK), bf16),
        in_specs=[IN_SMEM] + [IN_VMEM] * 4,
        out_specs=IN_VMEM,
        compiler_params=grant(6),
        name="project",
    )(place, near(rows_own), near(rows_other), near(right_cols), col_flip)
    partial_cols = pl.pallas_call(
        whiten_kernel,
        out_shape=pltpu.VMEM((ROWS, 2 * GROUP_ROWS, BLOCK), bf16),
        in_specs=[IN_SMEM] + [IN_VMEM] * 6,
        out_specs=IN_VMEM,
        scratch_shapes=[
            pltpu.VMEM((DM, BLOCK), f32),
            pltpu.VMEM((RADIX, 2 * INNER, BLOCK), f32),
        ],
        compiler_params=grant(16),
        name="whiten",
    )(place, near(tile), near(left_own), near(left_other), row_flip, column_table, twiddles)
    partial_rows = lax.all_to_all(partial_cols, ROW_AXES, 0, 0, tiled=True)

    row_table, turns = row_tables()
    picked = pl.pallas_call(
        spectrum_kernel,
        out_shape=pltpu.VMEM((list_len, 2 * BLOCK), bf16),
        in_specs=[IN_VMEM] * 5,
        out_specs=IN_VMEM,
        scratch_shapes=[pltpu.VMEM((NYC, GROUP_ROWS, 2 * BLOCK), f32)],
        compiler_params=grant(12),
        name="spectrum",
    )(near(partial_rows), near(cross), turns, row_table, wanted)

    entries = lax.all_to_all(
        jnp.broadcast_to(picked[None], (NE,) + picked.shape), "e", 0, 0, tiled=True
    ).reshape(NE * list_len, 2 * BLOCK)
    place = jnp.arange(ROWS * capacity, dtype=jnp.int32)[:, None] == position[None, :]
    outgoing = dot(place.astype(bf16), entries).astype(bf16)
    outgoing = outgoing.reshape(ROWS, capacity, 2 * BLOCK)
    arrived = lax.all_to_all(outgoing, ROW_AXES, 0, 0, tiled=True)
    return arrived.astype(f32)[None, None]


def solution(mesh):
    split = Mesh(mesh.devices.reshape(NZ, NY, NC, NE), ("z", "y", "c", "e"))
    in_specs = (
        P(None, "e", ROW_AXES, None),
        P(ROW_AXES, "e"),
        P(ROW_AXES + ("e",), None),
        P(),
        P(),
        P(None, ROW_AXES, "e", None),
        P(None, ROW_AXES, None, None, None),
    )
    out_specs = P(None, ROW_AXES, None, None, None)
    return jax.shard_map(shards, mesh=split, in_specs=in_specs, out_specs=out_specs, check_vma=False)
```

```python
import math

import jax
import jax.numpy as jnp
import numpy as np
from jax import lax
from jax.experimental import pallas as pl
from jax.experimental.pallas import tpu as pltpu
from jax.sharding import Mesh
from jax.sharding import PartitionSpec as P


DM = 2048
BLOCK = 128
NZ, NY, NC, NE = 8, 8, 2, 4
NYC = NY * NC
ROWS = NZ * NYC
GROUP_ROWS = DM // ROWS
TILE_ROWS = DM // NZ
RADIX = 8
INNER = DM // RADIX
ROOT_HALF = math.sqrt(0.5)

f32 = jnp.float32
bf16 = jnp.bfloat16
ROW_AXES = ("z", "y", "c")
IN_VMEM = pl.BlockSpec(memory_space=pltpu.VMEM)
IN_SMEM = pl.BlockSpec(memory_space=pltpu.SMEM)


def split_table(table):
    high = table.astype(bf16)
    low = (table - high.astype(np.float64)).astype(bf16)
    return [high, low]


def split_values(values):
    high = values.astype(bf16)
    return [high, (values - high.astype(f32)).astype(bf16)]


def dft_angles(rows, cols, length):
    return 2.0 * math.pi * ((np.arange(rows)[:, None] * np.arange(cols)[None, :]) % length) / length


def column_tables():
    angles = dft_angles(INNER, INNER, INNER)
    high, low = split_table(np.concatenate([np.cos(angles), -np.sin(angles)], axis=0))
    angles = dft_angles(INNER, RADIX, DM)
    twiddles = np.concatenate([np.cos(angles), -np.sin(angles)], axis=1).astype(np.float32)
    return np.concatenate([high, low, high], axis=1), twiddles


def row_tables():
    angles = dft_angles(BLOCK, BLOCK, BLOCK)
    real, imag = np.cos(angles), -np.sin(angles)
    full = np.concatenate(
        [np.concatenate([real, imag], axis=1), np.concatenate([-imag, real], axis=1)], axis=0
    )
    high, low = split_table(full)
    angles = dft_angles(NYC, BLOCK, DM)
    twiddles = np.stack([np.cos(angles), -np.sin(angles)]).astype(np.float32)
    return np.concatenate([high, low, high], axis=0), twiddles.reshape(2, NYC, 1, BLOCK)


def add(a, b):
    return (a[0] + b[0], a[1] + b[1])


def sub(a, b):
    return (a[0] - b[0], a[1] - b[1])


def mul(a, b):
    return (a[0] * b[0] - a[1] * b[1], a[0] * b[1] + a[1] * b[0])


def minus_i(a):
    return (a[1], -a[0])


def fft4(a, b, c, d):
    even, odd = add(a, c), sub(a, c)
    even2, odd2 = add(b, d), minus_i(sub(b, d))
    return [add(even, even2), add(odd, odd2), sub(even, even2), sub(odd, odd2)]


def fft8(terms):
    even = fft4(terms[0], terms[2], terms[4], terms[6])
    odd = fft4(terms[1], terms[3], terms[5], terms[7])
    one = ((odd[1][0] + odd[1][1]) * ROOT_HALF, (odd[1][1] - odd[1][0]) * ROOT_HALF)
    three = ((odd[3][1] - odd[3][0]) * ROOT_HALF, (odd[3][0] + odd[3][1]) * -ROOT_HALF)
    turned = [odd[0], one, minus_i(odd[2]), three]
    return [add(e, o) for e, o in zip(even, turned)] + [sub(e, o) for e, o in zip(even, turned)]


def fft16(terms):
    inner = [fft4(*[terms[4 * a + b] for a in range(4)]) for b in range(4)]
    out = [None] * 16
    for first in range(4):
        column = []
        for b in range(4):
            turn = -2.0 * math.pi * b * first / 16
            value = inner[b][first]
            if b * first:
                cos, sin = math.cos(turn), math.sin(turn)
                value = (value[0] * cos - value[1] * sin, value[0] * sin + value[1] * cos)
            column.append(value)
        for second, value in enumerate(fft4(*column)):
            out[first + 4 * second] = value
    return out


def dot(a, b):
    return jnp.dot(a, b, preferred_element_type=f32)


def deal_kernel(right_far, left_far, out, right, left, arrived):
    copies = [
        pltpu.make_async_copy(right_far, right, arrived.at[0]),
        pltpu.make_async_copy(left_far, left, arrived.at[1]),
    ]
    for copy in copies:
        copy.start()
    for copy in copies:
        copy.wait()
    quarter = GROUP_ROWS // NE
    width = right.shape[1]
    pack = BLOCK // NE
    column = lax.broadcasted_iota(jnp.int32, (width, width), 0)
    target = lax.broadcasted_iota(jnp.int32, (width, width), 1)
    order = target == pack * (column % NYC) + column // NYC
    sorted_cols = dot(right[...], jnp.where(order, 1.0, 0.0).astype(bf16))
    tail = left[...].astype(f32)
    tail = jnp.concatenate([tail, tail], axis=0)
    shape = (2 * quarter, BLOCK)
    upper = lax.broadcasted_iota(jnp.int32, shape, 0) < quarter
    lane_group = lax.broadcasted_iota(jnp.int32, shape, 1) // pack
    for tile in range(width // BLOCK):
        lanes = slice(tile * BLOCK, (tile + 1) * BLOCK)
        row_groups = []
        for half in range(2):
            value = sorted_cols[2 * quarter * half : 2 * quarter * (half + 1), lanes]
            row_groups += [value, pltpu.roll(value, quarter, axis=0)]
        for group in range(NE):
            yc = tile * NE + group
            piece = None
            for p in range(NE):
                moved = row_groups[p]
                if p != group:
                    moved = pltpu.roll(moved, (pack * (p - group)) % BLOCK, axis=1)
                piece = moved if piece is None else jnp.where(lane_group == p, moved, piece)
            for z in range(NZ):
                zc = z * NC + yc % NC
                both = jnp.where(upper, piece, tail[:, zc * BLOCK : (zc + 1) * BLOCK])
                out[z * NYC + yc] = both.astype(bf16)


def arrange_kernel(place, own, first_shared, second_shared, third_shared, right, left, pieces):
    for step, piece in enumerate((own, first_shared, second_shared, third_shared)):
        pieces[(place[0] + NE - step) % NE] = piece[...]
    quarter = GROUP_ROWS // NE
    pack = BLOCK // NE
    shape = (ROWS, 2 * quarter, BLOCK)
    first = lax.broadcasted_iota(jnp.int32, shape, 1) < quarter
    lane_group = lax.broadcasted_iota(jnp.int32, shape, 2) // pack
    values = [pieces[e].astype(f32) for e in range(NE)]
    unpacked = []
    for p in range(NE):
        rows = None
        for e in range(NE):
            moved = values[e]
            if e != p:
                moved = pltpu.roll(moved, (pack * (e - p)) % BLOCK, axis=2)
            rows = moved if rows is None else jnp.where(lane_group == e, moved, rows)
        unpacked.append(rows)
    rights, lefts = [], []
    for e in range(0, NE, 2):
        rights.append(jnp.where(first, unpacked[e], pltpu.roll(unpacked[e + 1], quarter, axis=1)))
        lefts.append(jnp.where(first, pltpu.roll(values[e], quarter, axis=1), values[e + 1]))
    right[...] = jnp.concatenate(rights, axis=1).astype(bf16)
    left[...] = jnp.concatenate(lefts, axis=1).astype(bf16)


def project_kernel(place, own, other, right, col_flip, out):
    factor = right[...].reshape(DM, BLOCK)
    for side, rows in enumerate((own, other)):
        part = dot(rows[...].reshape(TILE_ROWS // NC, DM), factor) * col_flip[...]
        part = part.astype(bf16).reshape(NY, GROUP_ROWS, BLOCK)
        for k in range(NY):
            from_c = place[1] if side == 0 else 1 - place[1]
            start = pl.multiple_of(GROUP_ROWS * (NC * k + from_c), GROUP_ROWS)
            out[pl.ds(start, GROUP_ROWS), :] = part[k]


def whiten_kernel(place, tile, own, other, row_flip, table, twiddles, out, white, stage):
    left = jnp.concatenate([own[...].reshape(DM, BLOCK), other[...].reshape(DM, BLOCK)], axis=1)
    half = TILE_ROWS // NC
    starts = [pl.multiple_of(half * side, half) for side in (place[1], 1 - place[1])]
    halves = [tile[pl.ds(start, half), :] for start in starts]
    white[...] = dot(left, jnp.concatenate(halves, axis=0)) * row_flip[...]
    for p in range(0, RADIX, 2):
        pair = [white[pl.ds(p + k, INNER, stride=RADIX), :] for k in range(2)]
        part = jnp.concatenate(pair, axis=1)
        part_high, part_low = split_values(part)
        both = dot(table[...], jnp.concatenate([part_high, part_high, part_low], axis=0))
        stage[p] = both[:, 0:BLOCK]
        stage[p + 1] = both[:, BLOCK:]

    def combine(step, carry):
        rows = pl.ds(pl.multiple_of(step * GROUP_ROWS, GROUP_ROWS), GROUP_ROWS)
        rows_imag = pl.ds(pl.multiple_of(INNER + step * GROUP_ROWS, GROUP_ROWS), GROUP_ROWS)
        factors = twiddles[rows, :]
        terms = [(stage[0, rows, :], stage[0, rows_imag, :])]
        for p in range(1, RADIX):
            factor = (factors[:, p : p + 1], factors[:, RADIX + p : RADIX + p + 1])
            terms.append(mul((stage[p, rows, :], stage[p, rows_imag, :]), factor))
        for k, value in enumerate(fft8(terms)):
            out[NYC * k + step, 0:GROUP_ROWS, :] = value[0].astype(bf16)
            out[NYC * k + step, GROUP_ROWS : 2 * GROUP_ROWS, :] = value[1].astype(bf16)
        return carry

    lax.fori_loop(0, INNER // GROUP_ROWS, combine, 0, unroll=4)


def spectrum_kernel(parts, cross, turns, table, wanted, out, mixed):
    for yc in range(NYC):
        total = parts[yc].astype(f32)
        for z in range(1, NZ):
            total = total + parts[z * NYC + yc].astype(f32)
        value = mul((total[0:GROUP_ROWS], total[GROUP_ROWS:]), (cross[0, yc], cross[1, yc]))
        mixed[yc, :, 0:BLOCK] = value[0]
        mixed[yc, :, BLOCK : 2 * BLOCK] = value[1]
    rows = mixed[...].reshape(NYC * GROUP_ROWS, 2 * BLOCK)
    rows_high, rows_low = split_values(rows)
    rows = dot(jnp.concatenate([rows_high, rows_high, rows_low], axis=1), table[...])
    rows = rows.reshape(NYC, GROUP_ROWS, 2 * BLOCK)
    terms = [
        mul((rows[yc, :, 0:BLOCK], rows[yc, :, BLOCK:]), (turns[0, yc], turns[1, yc]))
        for yc in range(NYC)
    ]
    blocks = [jnp.concatenate(value, axis=1).astype(bf16) for value in fft16(terms)]
    blocks = jnp.concatenate(blocks, axis=0)
    row = lax.broadcasted_iota(jnp.int32, (out.shape[0], NYC * GROUP_ROWS), 1)
    chosen = jnp.where(row == wanted[...], 1.0, 0.0).astype(bf16)
    out[...] = dot(chosen, blocks).astype(bf16)


def grant(mebibytes):
    return pltpu.CompilerParams(vmem_limit_bytes=mebibytes * 2**20)


def near(array):
    return pltpu.with_memory_space_constraint(array, pltpu.VMEM)


def far(array):
    return pltpu.with_memory_space_constraint(array, pltpu.HBM)


def shards(grads, right_inv, left_inv, row_signs, col_signs, listed, owners):
    z_id, y_id, c_id, e_id = (lax.axis_index(name) for name in ("z", "y", "c", "e"))
    yc_id = y_id * NC + c_id
    row_id = z_id * NYC + yc_id
    list_len = listed.shape[3]
    capacity = 2

    pieces = pl.pallas_call(
        deal_kernel,
        out_shape=jax.ShapeDtypeStruct((ROWS, 2 * GROUP_ROWS // NE, BLOCK), bf16),
        in_specs=[pl.BlockSpec(memory_space=pl.ANY)] * 2,
        scratch_shapes=[
            pltpu.VMEM(right_inv.shape, bf16),
            pltpu.VMEM(left_inv.shape, bf16),
            pltpu.SemaphoreType.DMA((2,)),
        ],
        compiler_params=grant(8),
        name="deal",
    )(far(right_inv), far(left_inv))
    pieces = lax.all_to_all(pieces, ROW_AXES, 0, 0, tiled=True)
    shared = [
        lax.ppermute(pieces, "e", [(i, (i + step) % NE) for i in range(NE)])
        for step in range(1, NE)
    ]
    rows_own = jnp.broadcast_to(grads.reshape(1, GROUP_ROWS, DM), (NY, GROUP_ROWS, DM))
    rows_own = lax.all_to_all(rows_own, "y", 0, 0, tiled=True)
    swap = [(0, 1), (1, 0)]
    rows_other = lax.ppermute(rows_own, "c", swap)
    place = jnp.stack([e_id, c_id])
    factor_shape = pltpu.VMEM((ROWS, GROUP_ROWS, BLOCK), bf16)
    right_cols, left_own = pl.pallas_call(
        arrange_kernel,
        out_shape=(factor_shape, factor_shape),
        in_specs=[IN_SMEM] + [IN_VMEM] * NE,
        out_specs=(IN_VMEM, IN_VMEM),
        scratch_shapes=[pltpu.VMEM((NE, ROWS, 2 * GROUP_ROWS // NE, BLOCK), bf16)],
        compiler_params=grant(12),
        name="arrange",
    )(place, *[near(piece) for piece in [pieces] + shared])
    left_other = lax.ppermute(left_own, "c", swap)
    row_bits = lax.dynamic_index_in_dim(row_signs[0], e_id, 0, keepdims=False)
    row_flip = (1 - 2 * row_bits).astype(f32)[:, None]
    col_bits = lax.dynamic_index_in_dim(col_signs[0], e_id, 0, keepdims=False)
    col_bits = col_bits.reshape(BLOCK, NYC)
    own_col = jnp.arange(NYC, dtype=jnp.int32) == yc_id
    col_bits = jnp.sum(jnp.where(own_col[None, :], col_bits, 0), axis=1)[None, :]
    col_flip = (1 - 2 * col_bits).astype(f32)
    spectrum_rows = row_id * GROUP_ROWS + jnp.arange(GROUP_ROWS, dtype=jnp.int32)
    columns = jnp.arange(NYC, dtype=jnp.int32)[:, None] + NYC * jnp.arange(BLOCK, dtype=jnp.int32)
    columns = columns.reshape(NYC, 1, BLOCK)
    phase = spectrum_rows[None, :, None] * columns
    angle = phase.astype(f32) * (2.0 * math.pi / (DM * DM))
    cross = jnp.stack([jnp.cos(angle), -jnp.sin(angle)]) * (1.0 / DM)
    local_ids = listed[0, 0, 0] - row_id * (GROUP_ROWS * NYC)
    wanted = (local_ids % NYC) * GROUP_ROWS + local_ids // NYC
    wanted = wanted[:, None]
    owner_ids = owners[0, 0, :, :, 0].reshape(-1)
    order = jnp.arange(NE * list_len, dtype=jnp.int32)
    same = (owner_ids[:, None] == owner_ids[None, :]) & (order[:, None] < order[None, :])
    position = owner_ids * capacity + jnp.sum(same.astype(jnp.int32), axis=0)
    column_table, twiddles = column_tables()
    tile = pl.pallas_call(
        project_kernel,
        out_shape=pltpu.VMEM((TILE_ROWS, BLOCK), bf16),
        in_specs=[IN_SMEM] + [IN_VMEM] * 4,
        out_specs=IN_VMEM,
        compiler_params=grant(6),
        name="project",
    )(place, near(rows_own), near(rows_other), near(right_cols), col_flip)
    partial_cols = pl.pallas_call(
        whiten_kernel,
        out_shape=pltpu.VMEM((ROWS, 2 * GROUP_ROWS, BLOCK), bf16),
        in_specs=[IN_SMEM] + [IN_VMEM] * 6,
        out_specs=IN_VMEM,
        scratch_shapes=[
            pltpu.VMEM((DM, BLOCK), f32),
            pltpu.VMEM((RADIX, 2 * INNER, BLOCK), f32),
        ],
        compiler_params=grant(16),
        name="whiten",
    )(place, near(tile), near(left_own), near(left_other), row_flip, column_table, twiddles)
    partial_rows = lax.all_to_all(partial_cols, ROW_AXES, 0, 0, tiled=True)

    row_table, turns = row_tables()
    picked = pl.pallas_call(
        spectrum_kernel,
        out_shape=pltpu.VMEM((list_len, 2 * BLOCK), bf16),
        in_specs=[IN_VMEM] * 5,
        out_specs=IN_VMEM,
        scratch_shapes=[pltpu.VMEM((NYC, GROUP_ROWS, 2 * BLOCK), f32)],
        compiler_params=grant(12),
        name="spectrum",
    )(near(partial_rows), near(cross), turns, row_table, wanted)

    entries = lax.all_to_all(
        jnp.broadcast_to(picked[None], (NE,) + picked.shape), "e", 0, 0, tiled=True
    ).reshape(NE * list_len, 2 * BLOCK)
    place = jnp.arange(ROWS * capacity, dtype=jnp.int32)[:, None] == position[None, :]
    outgoing = dot(place.astype(bf16), entries).astype(bf16)
    outgoing = outgoing.reshape(ROWS, capacity, 2 * BLOCK)
    arrived = lax.all_to_all(outgoing, ROW_AXES, 0, 0, tiled=True)
    return arrived.astype(f32)[None, None]


def solution(mesh):
    split = Mesh(mesh.devices.reshape(NZ, NY, NC, NE), ("z", "y", "c", "e"))
    in_specs = (
        P(None, "e", ROW_AXES, None),
        P(ROW_AXES, "e"),
        P(ROW_AXES + ("e",), None),
        P(),
        P(),
        P(None, ROW_AXES, "e", None),
        P(None, ROW_AXES, None, None, None),
    )
    out_specs = P(None, ROW_AXES, None, None, None)
    return jax.shard_map(shards, mesh=split, in_specs=in_specs, out_specs=out_specs, check_vma=False)
```

```python
import math

import jax
import jax.numpy as jnp
import numpy as np
from jax import lax
from jax.experimental import pallas as pl
from jax.experimental.pallas import tpu as pltpu
from jax.sharding import Mesh
from jax.sharding import PartitionSpec as P


DM = 2048
BLOCK = 128
NZ, NY, NC, NE = 8, 8, 2, 4
NYC = NY * NC
ROWS = NZ * NYC
GROUP_ROWS = DM // ROWS
TILE_ROWS = DM // NZ
RADIX = 8
INNER = DM // RADIX
PITCH = RADIX + 1
ROOT_HALF = math.sqrt(0.5)

f32 = jnp.float32
bf16 = jnp.bfloat16
ROW_AXES = ("z", "y", "c")
IN_VMEM = pl.BlockSpec(memory_space=pltpu.VMEM)
IN_SMEM = pl.BlockSpec(memory_space=pltpu.SMEM)


def split_table(table):
    high = table.astype(bf16)
    low = (table - high.astype(np.float64)).astype(bf16)
    return [high, low]


def split_values(values):
    high = values.astype(bf16)
    return [high, (values - high.astype(f32)).astype(bf16)]


def dft_angles(rows, cols, length):
    return 2.0 * math.pi * ((np.arange(rows)[:, None] * np.arange(cols)[None, :]) % length) / length


def column_tables():
    angles = dft_angles(INNER, INNER, INNER)
    high, low = split_table(np.concatenate([np.cos(angles), -np.sin(angles)], axis=0))
    angles = dft_angles(INNER, RADIX, DM)
    twiddles = np.concatenate([np.cos(angles), -np.sin(angles)], axis=1).astype(np.float32)
    return np.concatenate([high, low, high], axis=1), twiddles


def row_tables():
    angles = dft_angles(BLOCK, BLOCK, BLOCK)
    real, imag = np.cos(angles), -np.sin(angles)
    full = np.concatenate(
        [np.concatenate([real, imag], axis=1), np.concatenate([-imag, real], axis=1)], axis=0
    )
    high, low = split_table(full)
    angles = dft_angles(NYC, BLOCK, DM)
    twiddles = np.stack([np.cos(angles), -np.sin(angles)]).astype(np.float32)
    return np.concatenate([high, low, high], axis=0), twiddles.reshape(2, NYC, 1, BLOCK)


def add(a, b):
    return (a[0] + b[0], a[1] + b[1])


def sub(a, b):
    return (a[0] - b[0], a[1] - b[1])


def mul(a, b):
    return (a[0] * b[0] - a[1] * b[1], a[0] * b[1] + a[1] * b[0])


def minus_i(a):
    return (a[1], -a[0])


def fft4(a, b, c, d):
    even, odd = add(a, c), sub(a, c)
    even2, odd2 = add(b, d), minus_i(sub(b, d))
    return [add(even, even2), add(odd, odd2), sub(even, even2), sub(odd, odd2)]


def fft8(terms):
    even = fft4(terms[0], terms[2], terms[4], terms[6])
    odd = fft4(terms[1], terms[3], terms[5], terms[7])
    one = ((odd[1][0] + odd[1][1]) * ROOT_HALF, (odd[1][1] - odd[1][0]) * ROOT_HALF)
    three = ((odd[3][1] - odd[3][0]) * ROOT_HALF, (odd[3][0] + odd[3][1]) * -ROOT_HALF)
    turned = [odd[0], one, minus_i(odd[2]), three]
    return [add(e, o) for e, o in zip(even, turned)] + [sub(e, o) for e, o in zip(even, turned)]


def fft16(terms):
    inner = [fft4(*[terms[4 * a + b] for a in range(4)]) for b in range(4)]
    out = [None] * 16
    for first in range(4):
        column = []
        for b in range(4):
            turn = -2.0 * math.pi * b * first / 16
            value = inner[b][first]
            if b * first:
                cos, sin = math.cos(turn), math.sin(turn)
                value = (value[0] * cos - value[1] * sin, value[0] * sin + value[1] * cos)
            column.append(value)
        for second, value in enumerate(fft4(*column)):
            out[first + 4 * second] = value
    return out


def dot(a, b):
    return jnp.dot(a, b, preferred_element_type=f32)


def deal_kernel(right_far, left_far, out, right, left, arrived):
    copies = [
        pltpu.make_async_copy(right_far, right, arrived.at[0]),
        pltpu.make_async_copy(left_far, left, arrived.at[1]),
    ]
    for copy in copies:
        copy.start()
    for copy in copies:
        copy.wait()
    quarter = GROUP_ROWS // NE
    width = right.shape[1]
    pack = BLOCK // NE
    column = lax.broadcasted_iota(jnp.int32, (width, width), 0)
    target = lax.broadcasted_iota(jnp.int32, (width, width), 1)
    order = target == pack * (column % NYC) + column // NYC
    sorted_cols = dot(right[...], jnp.where(order, 1.0, 0.0).astype(bf16))
    tail = left[...].astype(f32)
    tail = jnp.concatenate([tail, tail], axis=0)
    shape = (2 * quarter, BLOCK)
    upper = lax.broadcasted_iota(jnp.int32, shape, 0) < quarter
    lane_group = lax.broadcasted_iota(jnp.int32, shape, 1) // pack
    for tile in range(width // BLOCK):
        lanes = slice(tile * BLOCK, (tile + 1) * BLOCK)
        row_groups = []
        for half in range(2):
            value = sorted_cols[2 * quarter * half : 2 * quarter * (half + 1), lanes]
            row_groups += [value, pltpu.roll(value, quarter, axis=0)]
        for group in range(NE):
            yc = tile * NE + group
            piece = None
            for p in range(NE):
                moved = row_groups[p]
                if p != group:
                    moved = pltpu.roll(moved, (pack * (p - group)) % BLOCK, axis=1)
                piece = moved if piece is None else jnp.where(lane_group == p, moved, piece)
            for z in range(NZ):
                zc = z * NC + yc % NC
                both = jnp.where(upper, piece, tail[:, zc * BLOCK : (zc + 1) * BLOCK])
                out[z * NYC + yc] = both.astype(bf16)


def arrange_kernel(place, own, first_shared, second_shared, third_shared, right, left, pieces):
    for step, piece in enumerate((own, first_shared, second_shared, third_shared)):
        pieces[(place[0] + NE - step) % NE] = piece[...]
    quarter = GROUP_ROWS // NE
    pack = BLOCK // NE
    shape = (ROWS, 2 * quarter, BLOCK)
    first = lax.broadcasted_iota(jnp.int32, shape, 1) < quarter
    lane_group = lax.broadcasted_iota(jnp.int32, shape, 2) // pack
    values = [pieces[e].astype(f32) for e in range(NE)]
    unpacked = []
    for p in range(NE):
        rows = None
        for e in range(NE):
            moved = values[e]
            if e != p:
                moved = pltpu.roll(moved, (pack * (e - p)) % BLOCK, axis=2)
            rows = moved if rows is None else jnp.where(lane_group == e, moved, rows)
        unpacked.append(rows)
    rights, lefts = [], []
    for e in range(0, NE, 2):
        rights.append(jnp.where(first, unpacked[e], pltpu.roll(unpacked[e + 1], quarter, axis=1)))
        lefts.append(jnp.where(first, pltpu.roll(values[e], quarter, axis=1), values[e + 1]))
    right[...] = jnp.concatenate(rights, axis=1).astype(bf16)
    left[...] = jnp.concatenate(lefts, axis=1).astype(bf16)


def project_kernel(place, own, other, right, col_flip, out):
    factor = right[...].reshape(DM, BLOCK)
    for side, rows in enumerate((own, other)):
        part = dot(rows[...].reshape(TILE_ROWS // NC, DM), factor) * col_flip[...]
        part = part.astype(bf16).reshape(NY, GROUP_ROWS, BLOCK)
        for k in range(NY):
            from_c = place[1] if side == 0 else 1 - place[1]
            start = pl.multiple_of(GROUP_ROWS * (NC * k + from_c), GROUP_ROWS)
            out[pl.ds(start, GROUP_ROWS), :] = part[k]


def whiten_kernel(place, tile, own, other, row_flip, table, twiddles, out, white, stage):
    left = jnp.concatenate([own[...].reshape(DM, BLOCK), other[...].reshape(DM, BLOCK)], axis=1)
    half = TILE_ROWS // NC
    starts = [pl.multiple_of(half * side, half) for side in (place[1], 1 - place[1])]
    halves = [tile[pl.ds(start, half), :] for start in starts]
    result = dot(left, jnp.concatenate(halves, axis=0)) * row_flip[...]
    for q in range(INNER):
        white[PITCH * q : PITCH * q + RADIX, :] = result[RADIX * q : RADIX * (q + 1)]
    for p in range(0, RADIX, 2):
        pair = [white[pl.ds(p + k, INNER, stride=PITCH), :] for k in range(2)]
        part = jnp.concatenate(pair, axis=1)
        part_high, part_low = split_values(part)
        both = dot(table[...], jnp.concatenate([part_high, part_high, part_low], axis=0))
        stage[p] = both[:, 0:BLOCK]
        stage[p + 1] = both[:, BLOCK:]

    def combine(step, carry):
        rows = pl.ds(pl.multiple_of(step * GROUP_ROWS, GROUP_ROWS), GROUP_ROWS)
        rows_imag = pl.ds(pl.multiple_of(INNER + step * GROUP_ROWS, GROUP_ROWS), GROUP_ROWS)
        factors = twiddles[rows, :]
        terms = [(stage[0, rows, :], stage[0, rows_imag, :])]
        for p in range(1, RADIX):
            factor = (factors[:, p : p + 1], factors[:, RADIX + p : RADIX + p + 1])
            terms.append(mul((stage[p, rows, :], stage[p, rows_imag, :]), factor))
        for k, value in enumerate(fft8(terms)):
            out[NYC * k + step, 0:GROUP_ROWS, :] = value[0].astype(bf16)
            out[NYC * k + step, GROUP_ROWS : 2 * GROUP_ROWS, :] = value[1].astype(bf16)
        return carry

    lax.fori_loop(0, INNER // GROUP_ROWS, combine, 0, unroll=4)


def spectrum_kernel(parts, cross, turns, table, wanted, out, mixed):
    for yc in range(NYC):
        total = parts[yc].astype(f32)
        for z in range(1, NZ):
            total = total + parts[z * NYC + yc].astype(f32)
        value = mul((total[0:GROUP_ROWS], total[GROUP_ROWS:]), (cross[0, yc], cross[1, yc]))
        mixed[yc, :, 0:BLOCK] = value[0]
        mixed[yc, :, BLOCK : 2 * BLOCK] = value[1]
    rows = mixed[...].reshape(NYC * GROUP_ROWS, 2 * BLOCK)
    rows_high, rows_low = split_values(rows)
    rows = dot(jnp.concatenate([rows_high, rows_high, rows_low], axis=1), table[...])
    rows = rows.reshape(NYC, GROUP_ROWS, 2 * BLOCK)
    terms = [
        mul((rows[yc, :, 0:BLOCK], rows[yc, :, BLOCK:]), (turns[0, yc], turns[1, yc]))
        for yc in range(NYC)
    ]
    blocks = [jnp.concatenate(value, axis=1).astype(bf16) for value in fft16(terms)]
    blocks = jnp.concatenate(blocks, axis=0)
    row = lax.broadcasted_iota(jnp.int32, (out.shape[0], NYC * GROUP_ROWS), 1)
    chosen = jnp.where(row == wanted[...], 1.0, 0.0).astype(bf16)
    out[...] = dot(chosen, blocks).astype(bf16)


def grant(mebibytes):
    return pltpu.CompilerParams(vmem_limit_bytes=mebibytes * 2**20)


def near(array):
    return pltpu.with_memory_space_constraint(array, pltpu.VMEM)


def far(array):
    return pltpu.with_memory_space_constraint(array, pltpu.HBM)


def shards(grads, right_inv, left_inv, row_signs, col_signs, listed, owners):
    z_id, y_id, c_id, e_id = (lax.axis_index(name) for name in ("z", "y", "c", "e"))
    yc_id = y_id * NC + c_id
    row_id = z_id * NYC + yc_id
    list_len = listed.shape[3]
    capacity = 2

    pieces = pl.pallas_call(
        deal_kernel,
        out_shape=jax.ShapeDtypeStruct((ROWS, 2 * GROUP_ROWS // NE, BLOCK), bf16),
        in_specs=[pl.BlockSpec(memory_space=pl.ANY)] * 2,
        scratch_shapes=[
            pltpu.VMEM(right_inv.shape, bf16),
            pltpu.VMEM(left_inv.shape, bf16),
            pltpu.SemaphoreType.DMA((2,)),
        ],
        compiler_params=grant(8),
        name="deal",
    )(far(right_inv), far(left_inv))
    pieces = lax.all_to_all(pieces, ROW_AXES, 0, 0, tiled=True)
    shared = [
        lax.ppermute(pieces, "e", [(i, (i + step) % NE) for i in range(NE)])
        for step in range(1, NE)
    ]
    rows_own = jnp.broadcast_to(grads.reshape(1, GROUP_ROWS, DM), (NY, GROUP_ROWS, DM))
    rows_own = lax.all_to_all(rows_own, "y", 0, 0, tiled=True)
    swap = [(0, 1), (1, 0)]
    rows_other = lax.ppermute(rows_own, "c", swap)
    place = jnp.stack([e_id, c_id])
    factor_shape = pltpu.VMEM((ROWS, GROUP_ROWS, BLOCK), bf16)
    right_cols, left_own = pl.pallas_call(
        arrange_kernel,
        out_shape=(factor_shape, factor_shape),
        in_specs=[IN_SMEM] + [IN_VMEM] * NE,
        out_specs=(IN_VMEM, IN_VMEM),
        scratch_shapes=[pltpu.VMEM((NE, ROWS, 2 * GROUP_ROWS // NE, BLOCK), bf16)],
        compiler_params=grant(12),
        name="arrange",
    )(place, *[near(piece) for piece in [pieces] + shared])
    left_other = lax.ppermute(left_own, "c", swap)
    row_bits = lax.dynamic_index_in_dim(row_signs[0], e_id, 0, keepdims=False)
    row_flip = (1 - 2 * row_bits).astype(f32)[:, None]
    col_bits = lax.dynamic_index_in_dim(col_signs[0], e_id, 0, keepdims=False)
    col_bits = col_bits.reshape(BLOCK, NYC)
    own_col = jnp.arange(NYC, dtype=jnp.int32) == yc_id
    col_bits = jnp.sum(jnp.where(own_col[None, :], col_bits, 0), axis=1)[None, :]
    col_flip = (1 - 2 * col_bits).astype(f32)
    spectrum_rows = row_id * GROUP_ROWS + jnp.arange(GROUP_ROWS, dtype=jnp.int32)
    columns = jnp.arange(NYC, dtype=jnp.int32)[:, None] + NYC * jnp.arange(BLOCK, dtype=jnp.int32)
    columns = columns.reshape(NYC, 1, BLOCK)
    phase = spectrum_rows[None, :, None] * columns
    angle = phase.astype(f32) * (2.0 * math.pi / (DM * DM))
    cross = jnp.stack([jnp.cos(angle), -jnp.sin(angle)]) * (1.0 / DM)
    local_ids = listed[0, 0, 0] - row_id * (GROUP_ROWS * NYC)
    wanted = (local_ids % NYC) * GROUP_ROWS + local_ids // NYC
    wanted = wanted[:, None]
    owner_ids = (owners + e_id // NE)[0, 0, :, :, 0].reshape(-1)
    order = jnp.arange(NE * list_len, dtype=jnp.int32)
    same = (owner_ids[:, None] == owner_ids[None, :]) & (order[:, None] < order[None, :])
    position = owner_ids * capacity + jnp.sum(same.astype(jnp.int32), axis=0)
    column_table, twiddles = column_tables()
    tile = pl.pallas_call(
        project_kernel,
        out_shape=pltpu.VMEM((TILE_ROWS, BLOCK), bf16),
        in_specs=[IN_SMEM] + [IN_VMEM] * 4,
        out_specs=IN_VMEM,
        compiler_params=grant(6),
        name="project",
    )(place, near(rows_own), near(rows_other), near(right_cols), col_flip)
    partial_cols = pl.pallas_call(
        whiten_kernel,
        out_shape=pltpu.VMEM((ROWS, 2 * GROUP_ROWS, BLOCK), bf16),
        in_specs=[IN_SMEM] + [IN_VMEM] * 6,
        out_specs=IN_VMEM,
        scratch_shapes=[
            pltpu.VMEM((PITCH * INNER, BLOCK), f32),
            pltpu.VMEM((RADIX, 2 * INNER, BLOCK), f32),
        ],
        compiler_params=grant(16),
        name="whiten",
    )(place, near(tile), near(left_own), near(left_other), row_flip, column_table, twiddles)
    partial_rows = lax.all_to_all(partial_cols, ROW_AXES, 0, 0, tiled=True)

    row_table, turns = row_tables()
    picked = pl.pallas_call(
        spectrum_kernel,
        out_shape=pltpu.VMEM((list_len, 2 * BLOCK), bf16),
        in_specs=[IN_VMEM] * 5,
        out_specs=IN_VMEM,
        scratch_shapes=[pltpu.VMEM((NYC, GROUP_ROWS, 2 * BLOCK), f32)],
        compiler_params=grant(12),
        name="spectrum",
    )(near(partial_rows), near(cross), turns, row_table, wanted)

    entries = lax.all_to_all(
        jnp.broadcast_to(picked[None], (NE,) + picked.shape), "e", 0, 0, tiled=True
    ).reshape(NE * list_len, 2 * BLOCK)
    place = jnp.arange(ROWS * capacity, dtype=jnp.int32)[:, None] == position[None, :]
    outgoing = dot(place.astype(bf16), entries).astype(bf16)
    outgoing = outgoing.reshape(ROWS, capacity, 2 * BLOCK)
    arrived = lax.all_to_all(outgoing, ROW_AXES, 0, 0, tiled=True)
    return arrived.astype(f32)[None, None]


def solution(mesh):
    split = Mesh(mesh.devices.reshape(NZ, NY, NC, NE), ("z", "y", "c", "e"))
    in_specs = (
        P(None, "e", ROW_AXES, None),
        P(ROW_AXES, "e"),
        P(ROW_AXES + ("e",), None),
        P(),
        P(),
        P(None, ROW_AXES, "e", None),
        P(None, ROW_AXES, None, None, None),
    )
    out_specs = P(None, ROW_AXES, None, None, None)
    return jax.shard_map(shards, mesh=split, in_specs=in_specs, out_specs=out_specs, check_vma=False)
```
